256 devices in a mesh: section: 2 (over y_hi), segment: 8 (over x, core), fsdp: 16 (over z, y_lo).
Axes of the slice: x: 4, y: 4 (y_hi: 2, y_lo: 2; y = y_hi * 2 + y_lo), z: 8, core: 2. Of those that a mesh axis runs over, the one named last changes fastest.
Arguments:
- out_grad: bfloat16 [2, 16, 256, 6144], P(None, 'fsdp'), may hold values from -48 to 48
- queries: bfloat16 [2, 16, 256, 6144], P(None, 'fsdp', None, 'segment'), may hold values from -40 to 40
- enc_keys: bfloat16 [2, 16, 256, 6144], P(None, 'fsdp', None, 'segment'), may hold values from -4 to 4
- enc_values: bfloat16 [2, 16, 256, 6144], P(None, 'fsdp', None, 'segment'), may hold values from -6 to 6
- key_mask: int32 [2, 16, 256], P(None, 'fsdp'), may hold values from 0 to 1, as said below
- weights: bfloat16 [2, 2, 6144, 6144], P('section', None, 'fsdp', 'segment'), may hold values from -0.078125 to 0.078125
Outputs:
- grads: bfloat16 [2, 2, 16, 256, 6144], P('section', None, 'fsdp', None, 'segment')
The draws below stay inside these ranges and needn't reach their ends.
Inputs may be any that keep to these rules, and one draw needn't show every extreme that they name: `key_mask`: each row is 1 on a prefix of 128 or more positions and 0 after it; the first reaction of every microbatch has no padding.
All inputs are finite; a program needn't handle non-finite values.
Results may differ from the reference program's by a relative error of at most 0.014.
Values may be sent and summed in bfloat16 or wider, within the bound.
No kernel may reach another device: no remote copies, remote signals or barrier semaphores. Data moves between devices by JAX's collectives and lax.ppermute only.
A program may use at most 128 MiB of HBM per device.

```python
import jax
import jax.numpy as jnp
from jax import lax

D = 6144
HEADS = 48
HDIM = 128
LEN = 256
MB = 2
BATCH = 16
HEADS_DEV = 6
N_SEGMENT = 8


def query_key_pair(key):
    shaped = (MB, BATCH, LEN, HEADS, HDIM)
    key_draw = jnp.clip(jax.random.normal(jax.random.fold_in(key, 11), shaped, jnp.float32), -4.0, 4.0)
    query_draw = jnp.clip(jax.random.normal(jax.random.fold_in(key, 12), shaped, jnp.float32), -4.0, 4.0)
    return (query_draw.reshape(MB, BATCH, LEN, HEADS * HDIM), key_draw.reshape(MB, BATCH, LEN, HEADS * HDIM))


def draw_queries(key, part):
    return query_key_pair(key)[0].astype(jnp.bfloat16)


def draw_enc_keys(key, part):
    return query_key_pair(key)[1].astype(jnp.bfloat16)


def draw_key_mask(key, part):
    lengths = jax.random.randint(jax.random.fold_in(key, 21), (MB, BATCH), LEN // 2, LEN + 1)
    lengths = lengths.at[:, 0].set(LEN)
    position = jnp.arange(LEN)
    return (position[None, None, :] < lengths[:, :, None]).astype(jnp.int32)


def block_levels(key, extent, split, least, largest):
    loudness, own = 1.0, jax.random.fold_in(key, 6)
    for dim, shards_of in split:
        draws = jnp.exp(jax.random.uniform(jax.random.fold_in(own, dim), (shards_of,), jnp.float32, least / len(split), largest / len(split)))
        loudness = loudness * jnp.repeat(draws, extent[dim] // shards_of).reshape([-1 if axis == dim else 1 for axis in range(len(extent))])
    return loudness


def scatter_about(stream_key, shape, scale, bound, shards=(), held_as=jnp.bfloat16):
    values = jax.random.normal(stream_key, shape, jnp.float32) * scale
    if len(shards) > 0:
        values = block_levels(stream_key, shape, shards, -0.22, 0.18) * values
    return jnp.clip(values, min=-bound, max=bound).astype(held_as)


def setup_inputs(seed: int = 0) -> dict:
    seeds = jax.random.split(jax.random.key(seed), 7)
    out_grad = scatter_about(seeds[0], (MB, BATCH, LEN, D), 8.0, 48.0, ((1, 16),))
    queries = draw_queries(jax.random.fold_in(seeds[6], 71), 0)
    enc_keys = draw_enc_keys(jax.random.fold_in(seeds[6], 71), 0)
    enc_values = scatter_about(seeds[3], (MB, BATCH, LEN, HEADS * HDIM), 1.0, 6.0, ((1, 16), (3, 8)))
    key_mask = draw_key_mask(jax.random.fold_in(seeds[6], 71), 0)
    weights = scatter_about(seeds[5], (2, 2, D, HEADS * HDIM), D ** -0.5, 0.078125, ((0, 2), (2, 16), (3, 8)))
    return dict(out_grad=out_grad, queries=queries, enc_keys=enc_keys, enc_values=enc_values, key_mask=key_mask, weights=weights)


def attention_grads(items):
    ctx_grad, queries, enc_keys, enc_values, key_mask = items
    score_scale = HDIM ** -0.5
    query_all = queries.astype(jnp.float32)
    key_all = enc_keys.astype(jnp.float32)
    value_all = enc_values.astype(jnp.float32)
    grad_all = ctx_grad.astype(jnp.float32)
    scores = jnp.einsum("ihc,jhc->hij", query_all, key_all) * score_scale
    scores = jnp.where(key_mask[None, None, :] > 0, scores, -jnp.inf)
    row_top = jnp.max(scores, axis=-1, keepdims=True)
    exp_scores = jnp.exp(scores - row_top)
    probabilities = exp_scores / jnp.sum(exp_scores, axis=-1, keepdims=True)
    probs_half = lax.optimization_barrier(probabilities.astype(jnp.bfloat16)).astype(jnp.float32)
    prob_grad = jnp.einsum("ihc,jhc->hij", grad_all, value_all)
    center = jnp.sum(probabilities * prob_grad, axis=-1, keepdims=True)
    score_grad = lax.optimization_barrier((probabilities * (prob_grad - center)).astype(jnp.bfloat16)).astype(jnp.float32)
    query_grad = (jnp.einsum("hij,jhc->ihc", score_grad, key_all) * score_scale).astype(jnp.bfloat16)
    key_grad = (jnp.einsum("hij,ihc->jhc", score_grad, query_all) * score_scale).astype(jnp.bfloat16)
    value_grad = jnp.einsum("hij,ihc->jhc", probs_half, grad_all).astype(jnp.bfloat16)
    return query_grad, key_grad, value_grad


def project(grad_rows, weight_cols):
    return jnp.dot(grad_rows, weight_cols.T, preferred_element_type=jnp.float32)


def reference(out_grad, queries, enc_keys, enc_values, key_mask, weights):
    row_count = MB * BATCH * LEN
    feature_width = HEADS * HDIM
    ctx_grad = jnp.dot(out_grad.reshape(row_count, D), weights[1, 0], preferred_element_type=jnp.float32).astype(jnp.bfloat16)
    shaped = (MB * BATCH, LEN, HEADS, HDIM)
    query_grad, key_grad, value_grad = lax.map(attention_grads, (ctx_grad.reshape(shaped), queries.reshape(shaped), enc_keys.reshape(shaped), enc_values.reshape(shaped), key_mask.reshape(MB * BATCH, LEN)))
    query_grad = query_grad.reshape(row_count, feature_width)
    key_grad = key_grad.reshape(row_count, feature_width)
    value_grad = value_grad.reshape(row_count, feature_width)
    group_width = HEADS_DEV * HDIM
    dec_total = jnp.zeros((row_count, D), jnp.float32)
    enc_total = jnp.zeros((row_count, D), jnp.float32)
    for group_index in range(N_SEGMENT):
        low = group_index * group_width
        high = low + group_width
        dec_part = project(query_grad[:, low:high], weights[1, 1][:, low:high])
        enc_part = project(key_grad[:, low:high], weights[0, 0][:, low:high]) + project(value_grad[:, low:high], weights[0, 1][:, low:high])
        dec_total = dec_total + lax.optimization_barrier(dec_part.astype(jnp.bfloat16)).astype(jnp.float32)
        enc_total = enc_total + lax.optimization_barrier(enc_part.astype(jnp.bfloat16)).astype(jnp.float32)
    stacked = jnp.stack([enc_total, dec_total]).astype(jnp.bfloat16)
    return stacked.reshape(2, MB, BATCH, LEN, D)
```

```python
import jax
import jax.numpy as jnp
from jax import lax
from jax.sharding import PartitionSpec as P

HDIM = 128

Z_LINES = [[2 * z + half for z in range(8)] for half in range(2)]
DEC_SWAP = [(16 + f, 16 + (f ^ 1)) for f in range(16)]
ENC_SWAP = [(f, f ^ 1) for f in range(16)]
DEC_SELF = [(16 + f, 16 + f) for f in range(16)]
DEC_TO_ENC = [(16 + f, f ^ 1) for f in range(16)]
HALF_SWAP = [(f, f ^ 1) for f in range(16)]
CORE_SWAP = [(g, g ^ 1) for g in range(8)]
BOTH = ("section", "fsdp")


def attend(ctx_grad, queries, enc_keys, enc_values, key_mask):
    reaction_count, seq_length, local_width = queries.shape
    head_count = local_width // HDIM
    score_scale = HDIM ** (-0.5)
    shaped = (reaction_count, seq_length, head_count, HDIM)
    grad_heads = ctx_grad.reshape(shaped)
    query_heads = queries.reshape(shaped)
    key_heads = enc_keys.reshape(shaped)
    value_heads = enc_values.reshape(shaped)
    scores = (
        jnp.einsum("bihc,bjhc->bhij", query_heads, key_heads, preferred_element_type=jnp.float32)
        * score_scale
    )
    scores = jnp.where(key_mask[:, None, None, :] > 0, scores, -jnp.inf)
    row_top = jnp.max(scores, axis=-1, keepdims=True)
    exp_scores = jnp.exp(scores - row_top)
    probabilities = exp_scores / jnp.sum(exp_scores, axis=-1, keepdims=True)
    probs_half = probabilities.astype(jnp.bfloat16)
    prob_grad = jnp.einsum(
        "bihc,bjhc->bhij", grad_heads, value_heads, preferred_element_type=jnp.float32
    )
    center = jnp.sum(probabilities * prob_grad, axis=-1, keepdims=True)
    score_grad = (probabilities * (prob_grad - center)).astype(jnp.bfloat16)
    query_grad = (
        jnp.einsum("bhij,bjhc->bihc", score_grad, key_heads, preferred_element_type=jnp.float32)
        * score_scale
    ).astype(jnp.bfloat16)
    key_grad = (
        jnp.einsum("bhij,bihc->bjhc", score_grad, query_heads, preferred_element_type=jnp.float32)
        * score_scale
    ).astype(jnp.bfloat16)
    value_grad = jnp.einsum(
        "bhij,bihc->bjhc", probs_half, grad_heads, preferred_element_type=jnp.float32
    ).astype(jnp.bfloat16)
    flat = (reaction_count * seq_length, local_width)
    return (query_grad.reshape(flat), key_grad.reshape(flat), value_grad.reshape(flat))


def times_rows(grad_rows, weight_rows):
    return jnp.einsum(
        "ik,xnk->xin", grad_rows, weight_rows, preferred_element_type=jnp.float32
    )


def dot(left, right):
    return jnp.dot(left, right, preferred_element_type=jnp.float32)


def per_device(out_grad, queries, enc_keys, enc_values, key_mask, weights):
    decoder = lax.axis_index("section") == 1
    half = lax.axis_index("fsdp") % 2
    segment = lax.axis_index("segment")
    core = segment % 2
    chip = segment // 2
    micro_count, reaction_count, seq_length, feature_width = out_grad.shape
    local_width = queries.shape[3]
    shard_rows = weights.shape[2]
    batch = micro_count * reaction_count
    row_count = batch * seq_length
    flat = (batch, seq_length, local_width)

    def gathered(shard):
        return lax.all_gather(shard, "fsdp", axis=0, axis_index_groups=Z_LINES)

    first = gathered(weights[0, 0])
    first, second_shard = lax.optimization_barrier((first, weights[0, 1]))
    second = gathered(second_shard)

    queries = queries.reshape(flat)
    enc_keys = enc_keys.reshape(flat)
    enc_values = enc_values.reshape(flat)
    key_mask = key_mask.reshape(batch, seq_length)
    near = [
        lax.ppermute(value, BOTH, ENC_SWAP + DEC_SELF)
        for value in (queries, enc_keys, enc_values, key_mask)
    ]

    pieces = out_grad.reshape(row_count, 8, 2, shard_rows)
    own_part = jnp.where(half == 0, pieces[:, :, 0], pieces[:, :, 1])
    far_part = jnp.where(half == 0, pieces[:, :, 1], pieces[:, :, 0])
    sent = jnp.where(core == 0, far_part[:, :4], far_part[:, 4:]).reshape(row_count, 4 * shard_rows)
    came = lax.ppermute(sent, BOTH, DEC_SWAP)
    twin = lax.ppermute(came, "segment", CORE_SWAP)
    partner_part = jnp.where(
        core == 0,
        jnp.concatenate([came, twin], axis=1),
        jnp.concatenate([twin, came], axis=1),
    )
    first_rows = first.reshape(8 * shard_rows, local_width)
    partner_partial = dot(partner_part, first_rows).astype(jnp.bfloat16)
    came_partial = lax.ppermute(partner_partial, BOTH, DEC_SWAP)
    own_partial = dot(own_part.reshape(row_count, 8 * shard_rows), first_rows)
    ctx_grad = (own_partial + came_partial.astype(jnp.float32)).astype(jnp.bfloat16)

    ctx_near = lax.ppermute(ctx_grad, BOTH, DEC_TO_ENC)
    ctx_own = lax.ppermute(ctx_near, BOTH, ENC_SWAP)

    query_near, key_near, value_near = attend(jnp.where(decoder, ctx_grad, ctx_near), *near)
    query_far = lax.ppermute(query_near, BOTH, DEC_SWAP)
    _, key_own, value_own = attend(ctx_own, queries, enc_keys, enc_values, key_mask)

    first_pairs = first.reshape(4, 2, shard_rows, local_width)
    second_pairs = second.reshape(4, 2, shard_rows, local_width)

    def taken(pairs, which):
        return lax.dynamic_index_in_dim(pairs, which, axis=1, keepdims=False)

    keep_first, give_first = taken(first_pairs, core), taken(first_pairs, 1 - core)
    keep_second, give_second = taken(second_pairs, core), taken(second_pairs, 1 - core)

    def projected(on_first, on_second):
        give = times_rows(on_first, give_first) + times_rows(on_second, give_second)
        other = lax.ppermute(give.astype(jnp.bfloat16), "segment", CORE_SWAP)
        keep = times_rows(on_first, keep_first) + times_rows(on_second, keep_second)
        total = keep + other.astype(jnp.float32)
        halved = total.astype(jnp.bfloat16)
        result = lax.dynamic_index_in_dim(total, chip, axis=0, keepdims=False)
        for step in (2, 1, 3):
            block = lax.dynamic_index_in_dim(halved, (chip + step) % 4, axis=0, keepdims=False)
            pairs = [(2 * x + k, 2 * ((x + step) % 4) + k) for x in range(4) for k in range(2)]
            result = result + lax.ppermute(block, "segment", pairs).astype(jnp.float32)
        return result.astype(jnp.bfloat16)

    nothing = jnp.zeros_like(key_near)
    partner_out = projected(
        jnp.where(decoder, nothing, key_near), jnp.where(decoder, query_far, value_near)
    )
    from_partner = lax.ppermute(partner_out, "fsdp", HALF_SWAP)
    own_out = projected(
        jnp.where(decoder, nothing, key_own), jnp.where(decoder, query_near, value_own)
    )
    result = jnp.where(
        half == 0,
        jnp.concatenate([own_out, from_partner], axis=1),
        jnp.concatenate([from_partner, own_out], axis=1),
    )
    return result.reshape(1, micro_count, reaction_count, seq_length, 2 * shard_rows)


def solution(mesh):
    return jax.shard_map(
        per_device,
        mesh=mesh,
        in_specs=(
            P(None, "fsdp", None, None),
            P(None, "fsdp", None, "segment"),
            P(None, "fsdp", None, "segment"),
            P(None, "fsdp", None, "segment"),
            P(None, "fsdp", None),
            P("section", None, "fsdp", "segment"),
        ),
        out_specs=P("section", None, "fsdp", None, "segment"),
        check_vma=False,
    )
```

```python
import functools

import jax
import jax.numpy as jnp
from jax import lax
from jax.experimental import pallas as pl
from jax.experimental.pallas import tpu as pltpu
from jax.sharding import PartitionSpec as P


HDIM = 128

Z_LINES = [[2 * z + half for z in range(8)] for half in range(2)]
DEC_SWAP = [(16 + f, 16 + (f ^ 1)) for f in range(16)]
ENC_SWAP = [(f, f ^ 1) for f in range(16)]
DEC_TO_ENC = [(16 + f, f ^ 1) for f in range(16)]
HALF_SWAP = [(f, f ^ 1) for f in range(16)]
CORE_SWAP = [(g, g ^ 1) for g in range(8)]
BOTH = ("section", "fsdp")
STEPS = (2, 1, 3, 0)
F32 = jnp.float32
BF16 = jnp.bfloat16
NT = (((1,), (1,)), ((), ()))
TN = (((0,), (0,)), ((), ()))
NN = (((1,), (0,)), ((), ()))


def mm(left, right, dims):
    return lax.dot_general(left, right, dims, preferred_element_type=F32)


def cost(flops, bytes_accessed):
    return pl.CostEstimate(flops=flops, bytes_accessed=bytes_accessed, transcendentals=0)


def pick_kernel(where, source, target):
    target[...] = source[...]


def picked(source, columns, width):
    rows = source.shape[0]
    count = columns.shape[0]
    return pl.pallas_call(
        pick_kernel,
        grid_spec=pltpu.PrefetchScalarGridSpec(
            num_scalar_prefetch=1,
            grid=(count,),
            in_specs=[pl.BlockSpec((rows, width), lambda i, at: (0, at[i]))],
            out_specs=pl.BlockSpec((rows, width), lambda i, at: (0, i)),
        ),
        out_shape=jax.ShapeDtypeStruct((rows, count * width), source.dtype),
        cost_estimate=cost(0, 2 * rows * count * width * 2),
        name="pick",
    )(columns, source)


def far_kernel(core, came, twin, weight, out, acc):
    step = pl.program_id(0)

    @pl.when(step == 0)
    def _():
        acc[...] = jnp.zeros_like(acc)

    rows = jnp.where(core[0] == step // 2, came[...], twin[...])
    acc[...] += mm(rows, weight[...], NN)

    @pl.when(step == pl.num_programs(0) - 1)
    def _():
        out[...] = acc[...].astype(BF16)


def far_partial(core, came, twin, weight, micro, seq_length):
    depth, width = weight.shape
    piece = depth // 4
    rows = pl.BlockSpec((seq_length, piece), lambda j, core: (micro, j % 2))
    return pl.pallas_call(
        far_kernel,
        grid_spec=pltpu.PrefetchScalarGridSpec(
            num_scalar_prefetch=1,
            grid=(4,),
            in_specs=[rows, rows, pl.BlockSpec((piece, width), lambda j, core: (j, 0))],
            out_specs=pl.BlockSpec((seq_length, width), lambda j, core: (0, 0)),
            scratch_shapes=[pltpu.VMEM((seq_length, width), F32)],
        ),
        out_shape=jax.ShapeDtypeStruct((seq_length, width), BF16),
        cost_estimate=cost(2 * seq_length * depth * width, 2 * depth * width),
        name="far",
    )(core, came, twin, weight)


def near_kernel(half, low, high, weight, *outs):
    part = mm(jnp.concatenate([low[...], high[...]], axis=1), weight[...], NN)
    rows = part.shape[0] // len(outs)
    for micro, out in enumerate(outs):
        cut = part[micro * rows : (micro + 1) * rows]

        @pl.when(pl.program_id(0) == 0)
        def _():
            out[...] = cut

        @pl.when(pl.program_id(0) > 0)
        def _():
            out[...] += cut


def near_partial(half, grads, weight):
    row_count = grads.shape[0]
    depth, width = weight.shape
    piece = depth // 4
    return pl.pallas_call(
        near_kernel,
        grid_spec=pltpu.PrefetchScalarGridSpec(
            num_scalar_prefetch=1,
            grid=(4,),
            in_specs=[
                pl.BlockSpec((row_count, piece // 2), lambda j, half: (0, 4 * j + half[0])),
                pl.BlockSpec((row_count, piece // 2), lambda j, half: (0, 4 * j + 2 + half[0])),
                pl.BlockSpec((piece, width), lambda j, half: (j, 0)),
            ],
            out_specs=[pl.BlockSpec((row_count // 2, width), lambda j, half: (0, 0))] * 2,
        ),
        out_shape=[jax.ShapeDtypeStruct((row_count // 2, width), F32)] * 2,
        cost_estimate=cost(2 * row_count * depth * width, 2 * depth * width),
        name="near",
    )(half, grads, grads, weight)


def attend_kernel(heads, flags, held, sent, query, key, value, mask, dq, dk, dv):
    scale = HDIM ** (-0.5)
    here = mask[0] > 0

    @pl.when(flags[0] + flags[1] > 0)
    def _():
        for head in range(heads):
            cut = slice(head * HDIM, (head + 1) * HDIM)
            grad = jnp.where(flags[2] > 0, held[:, cut], sent[:, cut])
            q, k, v = query[:, cut], key[:, cut], value[:, cut]
            scores = jnp.where(here, mm(q, k, NT) * scale, -jnp.inf)
            raised = jnp.exp(scores - jnp.max(scores, axis=-1, keepdims=True))
            probs = raised * (1.0 / jnp.sum(raised, axis=-1, keepdims=True))
            prob_grad = mm(grad, v, NT)
            center = jnp.sum(probs * prob_grad, axis=-1, keepdims=True)
            score_grad = (probs * (prob_grad - center)).astype(BF16)

            @pl.when(flags[0] > 0)
            def _():
                dq[:, cut] = (mm(score_grad, k, NN) * scale).astype(BF16)

            @pl.when(flags[1] > 0)
            def _():
                dk[:, cut] = (mm(score_grad, q, TN) * scale).astype(BF16)
                dv[:, cut] = mm(probs.astype(BF16), grad, TN).astype(BF16)


def attend(flags, held, sent, query, key, value, mask, micro):
    seq_length, width = held.shape
    heads = 2
    wide = heads * HDIM
    one = pl.BlockSpec((seq_length, wide), lambda h, flags: (0, h))
    row = pl.BlockSpec((None, seq_length, wide), lambda h, flags: (micro, 0, h))
    out = jax.ShapeDtypeStruct((seq_length, width), BF16)
    return pl.pallas_call(
        functools.partial(attend_kernel, heads),
        grid_spec=pltpu.PrefetchScalarGridSpec(
            num_scalar_prefetch=1,
            grid=(width // wide,),
            in_specs=[
                one,
                one,
                row,
                row,
                row,
                pl.BlockSpec((1, 1, seq_length), lambda h, flags: (micro, 0, 0)),
            ],
            out_specs=[one, one, one],
        ),
        out_shape=[out, out, out],
        cost_estimate=cost(
            10 * seq_length * seq_length * width, 16 * seq_length * width
        ),
        name="attend",
    )(flags, held, sent, query, key, value, mask)


def products(flags, grads, first, second, put):
    dq, dk, dv = grads
    for micro in range(2):

        @pl.when(flags[0] > 0)
        def _():
            put(micro, mm(dq[micro][...], second[...], NT))

        @pl.when(flags[0] == 0)
        def _():
            put(micro, mm(dk[micro][...], first[...], NT) + mm(dv[micro][...], second[...], NT))


def give_kernel(at, flags, q0, q1, k0, k1, v0, v1, first, second, out):
    rows = q0.shape[0]

    def put(micro, value):
        out[micro * rows : (micro + 1) * rows, :] = value.astype(BF16)

    products(flags, ((q0, q1), (k0, k1), (v0, v1)), first, second, put)


def keep_kernel(at, flags, q0, q1, k0, k1, v0, v1, first, second, other, *outs):
    rows = q0.shape[0]

    def put(micro, value):
        cut = slice(micro * rows, (micro + 1) * rows)
        total = value + other[cut, :].astype(F32)
        for i, out in enumerate(outs):

            @pl.when(pl.program_id(0) == i)
            def _():
                out[cut, :] = total.astype(out.dtype)

    products(flags, ((q0, q1), (k0, k1), (v0, v1)), first, second, put)


def projected(at, flags, grads, first, second, other=None):
    rows, width = grads[0].shape
    shard = first.shape[1]
    whole = pl.BlockSpec((rows, width), lambda i, at, flags: (0, 0))
    weight = pl.BlockSpec((None, shard, width), lambda i, at, flags: (at[i], 0, 0))
    moving = pl.BlockSpec((None, 2 * rows, shard), lambda i, at, flags: (i, 0, 0))
    fixed = pl.BlockSpec((2 * rows, shard), lambda i, at, flags: (0, 0))
    if other is None:
        kernel, extra = give_kernel, ()
        out_specs = moving
        out_shape = jax.ShapeDtypeStruct((4, 2 * rows, shard), BF16)
    else:
        kernel, extra = keep_kernel, (other,)
        out_specs = [fixed] * 4
        out_shape = [jax.ShapeDtypeStruct((2 * rows, shard), t) for t in (BF16, BF16, BF16, F32)]
    return pl.pallas_call(
        kernel,
        grid_spec=pltpu.PrefetchScalarGridSpec(
            num_scalar_prefetch=2,
            grid=(4,),
            in_specs=[whole] * 6 + [weight] * 2 + [moving] * len(extra),
            out_specs=out_specs,
        ),
        out_shape=out_shape,
        cost_estimate=cost(2 * 2 * rows * 2 * width * 4 * shard, 2 * 2 * 4 * shard * width),
    )(at, flags, *grads, first, second, *extra)


def per_device(out_grad, queries, enc_keys, enc_values, key_mask, weights):
    decoder = lax.axis_index("section") == 1
    half = lax.axis_index("fsdp") % 2
    segment = lax.axis_index("segment")
    core = segment % 2
    chip = segment // 2
    micro_count, reaction_count, seq_length, feature_width = out_grad.shape
    local_width = queries.shape[3]
    shard_rows = weights.shape[2]
    row_count = micro_count * reaction_count * seq_length
    flat = (micro_count, seq_length, local_width)
    micros = range(micro_count)
    dec = decoder.astype(jnp.int32)

    def gathered(shard):
        return lax.all_gather(shard, "fsdp", axis=0, axis_index_groups=Z_LINES)

    grads = out_grad.reshape(row_count, feature_width)
    columns = 2 * (4 * core + jnp.arange(4, dtype=jnp.int32)) + 1 - half
    came = lax.ppermute(picked(grads, columns, shard_rows), BOTH, DEC_SWAP)
    twin = lax.ppermute(came, "segment", CORE_SWAP)

    own = (
        queries.reshape(flat),
        enc_keys.reshape(flat),
        enc_values.reshape(flat),
        key_mask.reshape(micro_count, 1, seq_length),
    )
    came_near = tuple(lax.ppermute(value, BOTH, ENC_SWAP) for value in own)

    first = gathered(weights[0, 0])
    first, second_shard, came_near, came, twin = lax.optimization_barrier(
        (first, weights[0, 1], came_near, came, twin)
    )
    second = gathered(second_shard)
    near = [jnp.where(decoder, mine, other) for mine, other in zip(own, came_near)]

    first_rows = first.reshape(8 * shard_rows, local_width)
    far = [
        lax.ppermute(
            far_partial(core[None], came, twin, first_rows, micro, seq_length), BOTH, DEC_SWAP
        )
        for micro in micros
    ]
    own_partial = near_partial(half[None], grads, first_rows)
    ctx, ctx_near, ctx_own = [], [], []
    for micro in micros:
        part = far[micro]
        if micro > 0:
            part, ctx[-1] = lax.optimization_barrier((part, ctx[-1]))
        ctx.append((own_partial[micro] + part.astype(F32)).astype(BF16))
        ctx_near.append(lax.ppermute(ctx[micro], BOTH, DEC_TO_ENC))
        ctx_own.append(lax.ppermute(ctx_near[micro], BOTH, ENC_SWAP))

    near_flags = jnp.stack([dec, 1 - dec, dec])
    own_flags = jnp.stack([0 * dec, 1 - dec, 0 * dec])

    def attended(flags, held, sent, operands):
        grads = []
        for micro in micros:
            came = sent[micro]
            if micro > 0:
                came, grads[-1] = lax.optimization_barrier((came, grads[-1]))
            grads.append(attend(flags, held[micro], came, *operands, micro))
        return zip(*grads)

    dq, dk, dv = attended(near_flags, ctx, ctx_near, near)
    far_dq = []
    for micro in micros:
        far_dq.append(lax.ppermute(dq[micro], BOTH, DEC_SWAP))
    _, own_dk, own_dv = attended(own_flags, ctx, ctx_own, own)

    places = 2 * ((chip + jnp.array(STEPS, jnp.int32)) % 4)
    keep_at, give_at = places + core, places + 1 - core

    second, own_dk, own_dv = lax.optimization_barrier((second, own_dk, own_dv))

    def chip_sums(grads):
        give = projected(give_at, dec[None], grads, first, second)
        other = lax.ppermute(give, "segment", CORE_SWAP)
        return projected(keep_at, dec[None], grads, first, second, other)

    def reduced(blocks, result):
        for step, block in zip(STEPS, blocks):
            pairs = [(2 * x + k, 2 * ((x + step) % 4) + k) for x in range(4) for k in range(2)]
            other = lax.ppermute(block, "segment", pairs)
            result = result + other.astype(F32)
        return result.astype(BF16)

    *blocks, block = chip_sums((*far_dq, *dk, *dv))
    own_grads, blocks = lax.optimization_barrier(((*dq, *own_dk, *own_dv), blocks))
    from_partner = lax.ppermute(reduced(blocks, block), "fsdp", HALF_SWAP)
    *blocks, block = chip_sums(own_grads)
    own_out = reduced(blocks, block)
    result = jnp.where(
        half == 0,
        jnp.concatenate([own_out, from_partner], axis=1),
        jnp.concatenate([from_partner, own_out], axis=1),
    )
    return result.reshape(1, micro_count, reaction_count, seq_length, 2 * shard_rows)


def solution(mesh):
    return jax.shard_map(
        per_device,
        mesh=mesh,
        in_specs=(
            P(None, "fsdp", None, None),
            P(None, "fsdp", None, "segment"),
            P(None, "fsdp", None, "segment"),
            P(None, "fsdp", None, "segment"),
            P(None, "fsdp", None),
            P("section", None, "fsdp", "segment"),
        ),
        out_specs=P("section", None, "fsdp", None, "segment"),
        check_vma=False,
    )
```

```python
import functools

import jax
import jax.numpy as jnp
from jax import lax
from jax.experimental import pallas as pl
from jax.experimental.pallas import tpu as pltpu
from jax.sharding import PartitionSpec as P


HDIM = 128

Z_LINES = [[2 * z + half for z in range(8)] for half in range(2)]
DEC_SWAP = [(16 + f, 16 + (f ^ 1)) for f in range(16)]
ENC_SWAP = [(f, f ^ 1) for f in range(16)]
DEC_TO_ENC = [(16 + f, f ^ 1) for f in range(16)]
HALF_SWAP = [(f, f ^ 1) for f in range(16)]
CORE_SWAP = [(g, g ^ 1) for g in range(8)]
BOTH = ("section", "fsdp")
STEPS = (2, 1, 3, 0)
F32 = jnp.float32
BF16 = jnp.bfloat16
NT = (((1,), (1,)), ((), ()))
TN = (((0,), (0,)), ((), ()))
NN = (((1,), (0,)), ((), ()))


def mm(left, right, dims):
    return lax.dot_general(left, right, dims, preferred_element_type=F32)


def cost(flops, bytes_accessed):
    return pl.CostEstimate(flops=flops, bytes_accessed=bytes_accessed, transcendentals=0)


def pick_kernel(where, source, target):
    target[...] = source[...]


def picked(source, columns, width):
    rows = source.shape[0]
    count = columns.shape[0]
    return pl.pallas_call(
        pick_kernel,
        grid_spec=pltpu.PrefetchScalarGridSpec(
            num_scalar_prefetch=1,
            grid=(count,),
            in_specs=[pl.BlockSpec((rows, width), lambda i, at: (0, at[i]))],
            out_specs=pl.BlockSpec((rows, width), lambda i, at: (0, i)),
        ),
        out_shape=jax.ShapeDtypeStruct((rows, count * width), source.dtype),
        cost_estimate=cost(0, 2 * rows * count * width * 2),
        name="pick",
    )(columns, source)


def far_kernel(core, came, twin, weight, low, high, acc):
    step = pl.program_id(0)

    @pl.when(step == 0)
    def _():
        acc[...] = jnp.zeros_like(acc)

    rows = jnp.where(core[0] == step // 2, came[...], twin[...])
    acc[...] += mm(rows, weight[...], NN)

    @pl.when(step == pl.num_programs(0) - 1)
    def _():
        rows = low.shape[0]
        low[...] = acc[:rows].astype(BF16)
        high[...] = acc[rows:].astype(BF16)


def far_partial(core, came, twin, weight):
    row_count = came.shape[0]
    depth, width = weight.shape
    piece = depth // 4
    rows = pl.BlockSpec((row_count, piece), lambda j, core: (0, j % 2))
    return pl.pallas_call(
        far_kernel,
        grid_spec=pltpu.PrefetchScalarGridSpec(
            num_scalar_prefetch=1,
            grid=(4,),
            in_specs=[rows, rows, pl.BlockSpec((piece, width), lambda j, core: (j, 0))],
            out_specs=[pl.BlockSpec((row_count // 2, width), lambda j, core: (0, 0))] * 2,
            scratch_shapes=[pltpu.VMEM((row_count, width), F32)],
        ),
        out_shape=[jax.ShapeDtypeStruct((row_count // 2, width), BF16)] * 2,
        cost_estimate=cost(2 * row_count * depth * width, 2 * depth * width),
        name="far",
    )(core, came, twin, weight)


def near_kernel(half, low, high, weight, *outs):
    part = mm(jnp.concatenate([low[...], high[...]], axis=1), weight[...], NN)
    rows = part.shape[0] // len(outs)
    for micro, out in enumerate(outs):
        cut = part[micro * rows : (micro + 1) * rows]

        @pl.when(pl.program_id(0) == 0)
        def _():
            out[...] = cut

        @pl.when(pl.program_id(0) > 0)
        def _():
            out[...] += cut


def near_partial(half, grads, weight):
    row_count = grads.shape[0]
    depth, width = weight.shape
    piece = depth // 4
    return pl.pallas_call(
        near_kernel,
        grid_spec=pltpu.PrefetchScalarGridSpec(
            num_scalar_prefetch=1,
            grid=(4,),
            in_specs=[
                pl.BlockSpec((row_count, piece // 2), lambda j, half: (0, 4 * j + half[0])),
                pl.BlockSpec((row_count, piece // 2), lambda j, half: (0, 4 * j + 2 + half[0])),
                pl.BlockSpec((piece, width), lambda j, half: (j, 0)),
            ],
            out_specs=[pl.BlockSpec((row_count // 2, width), lambda j, half: (0, 0))] * 2,
        ),
        out_shape=[jax.ShapeDtypeStruct((row_count // 2, width), F32)] * 2,
        cost_estimate=cost(2 * row_count * depth * width, 2 * depth * width),
        name="near",
    )(half, grads, grads, weight)


def attend_kernel(heads, flags, held, sent, query, key, value, mask, dq, dk, dv):
    scale = HDIM ** (-0.5)
    cuts = [slice(head * HDIM, (head + 1) * HDIM) for head in range(heads)]

    def grads_of(cut):
        grad = jnp.where(flags[2] > 0, held[:, cut], sent[:, cut])
        q, k, v = query[:, cut], key[:, cut], value[:, cut]
        scores = jnp.where(mask[...] > 0, mm(k, q, NT) * scale, -jnp.inf)
        raised = jnp.exp(scores - jnp.max(scores, axis=0, keepdims=True))
        probs = raised * (1.0 / jnp.sum(raised, axis=0, keepdims=True))
        prob_grad = mm(v, grad, NT)
        center = jnp.sum(probs * prob_grad, axis=0, keepdims=True)
        return grad, q, k, probs, (probs * (prob_grad - center)).astype(BF16)

    @pl.when(flags[0] > 0)
    def _():
        for cut in cuts:
            _, _, k, _, score_grad = grads_of(cut)
            dq[:, cut] = (mm(score_grad, k, TN) * scale).astype(BF16)

    @pl.when(flags[1] > 0)
    def _():
        for cut in cuts:
            grad, q, _, probs, score_grad = grads_of(cut)
            dk[:, cut] = (mm(score_grad, q, NN) * scale).astype(BF16)
            dv[:, cut] = mm(probs.astype(BF16), grad, NN).astype(BF16)


def attend(flags, held, sent, query, key, value, mask, micro):
    seq_length, width = held.shape
    heads = 2
    wide = heads * HDIM
    one = pl.BlockSpec((seq_length, wide), lambda h, flags: (0, h))
    row = pl.BlockSpec((None, seq_length, wide), lambda h, flags: (micro, 0, h))
    out = jax.ShapeDtypeStruct((seq_length, width), BF16)
    return pl.pallas_call(
        functools.partial(attend_kernel, heads),
        grid_spec=pltpu.PrefetchScalarGridSpec(
            num_scalar_prefetch=1,
            grid=(width // wide,),
            in_specs=[
                one,
                one,
                row,
                row,
                row,
                pl.BlockSpec((None, seq_length, 1), lambda h, flags: (micro, 0, 0)),
            ],
            out_specs=[one, one, one],
        ),
        out_shape=[out, out, out],
        cost_estimate=cost(
            10 * seq_length * seq_length * width, 16 * seq_length * width
        ),
        name="attend",
    )(flags, held, sent, query, key, value, mask)


def products(flags, grads, first, second, put):
    dq, dk, dv = [lambda pair=pair: jnp.concatenate([x[...] for x in pair]) for pair in grads]

    @pl.when(flags[0] > 0)
    def _():
        put(mm(dq(), second[...], NT))

    @pl.when(flags[0] == 0)
    def _():
        put(mm(dk(), first[...], NT) + mm(dv(), second[...], NT))


def give_kernel(at, flags, q0, q1, k0, k1, v0, v1, first, second, out):
    def put(value):
        out[...] = value.astype(BF16)

    products(flags, ((q0, q1), (k0, k1), (v0, v1)), first, second, put)


def keep_kernel(at, flags, q0, q1, k0, k1, v0, v1, first, second, other, *outs):
    def put(value):
        total = value + other[...].astype(F32)
        for i, out in enumerate(outs):

            @pl.when(pl.program_id(0) == i)
            def _():
                out[...] = total.astype(out.dtype)

    products(flags, ((q0, q1), (k0, k1), (v0, v1)), first, second, put)


def projected(at, flags, grads, first, second, other=None):
    rows, width = grads[0].shape
    shard = first.shape[1]
    whole = pl.BlockSpec((rows, width), lambda i, at, flags: (0, 0))
    weight = pl.BlockSpec((None, shard, width), lambda i, at, flags: (at[i], 0, 0))
    moving = pl.BlockSpec((None, 2 * rows, shard), lambda i, at, flags: (i, 0, 0))
    fixed = pl.BlockSpec((2 * rows, shard), lambda i, at, flags: (0, 0))
    if other is None:
        kernel, extra = give_kernel, ()
        out_specs = moving
        out_shape = jax.ShapeDtypeStruct((4, 2 * rows, shard), BF16)
    else:
        kernel, extra = keep_kernel, (other,)
        out_specs = [fixed] * 4
        out_shape = [jax.ShapeDtypeStruct((2 * rows, shard), t) for t in (BF16, BF16, BF16, F32)]
    return pl.pallas_call(
        kernel,
        grid_spec=pltpu.PrefetchScalarGridSpec(
            num_scalar_prefetch=2,
            grid=(4,),
            in_specs=[whole] * 6 + [weight] * 2 + [moving] * len(extra),
            out_specs=out_specs,
        ),
        out_shape=out_shape,
        cost_estimate=cost(2 * 2 * rows * 2 * width * 4 * shard, 2 * 2 * 4 * shard * width),
    )(at, flags, *grads, first, second, *extra)


def per_device(out_grad, queries, enc_keys, enc_values, key_mask, weights):
    decoder = lax.axis_index("section") == 1
    half = lax.axis_index("fsdp") % 2
    segment = lax.axis_index("segment")
    core = segment % 2
    chip = segment // 2
    micro_count, reaction_count, seq_length, feature_width = out_grad.shape
    local_width = queries.shape[3]
    shard_rows = weights.shape[2]
    row_count = micro_count * reaction_count * seq_length
    flat = (micro_count, seq_length, local_width)
    micros = range(micro_count)
    dec = decoder.astype(jnp.int32)

    def gathered(shard):
        return lax.all_gather(shard, "fsdp", axis=0, axis_index_groups=Z_LINES)

    grads = out_grad.reshape(row_count, feature_width)
    columns = 2 * (4 * core + jnp.arange(4, dtype=jnp.int32)) + 1 - half
    came = lax.ppermute(picked(grads, columns, shard_rows), BOTH, DEC_SWAP)
    twin = lax.ppermute(came, "segment", CORE_SWAP)

    own = (
        queries.reshape(flat),
        enc_keys.reshape(flat),
        enc_values.reshape(flat),
        key_mask.reshape(micro_count, 1, seq_length),
    )
    came_near = tuple(lax.ppermute(value, BOTH, ENC_SWAP) for value in own)

    first = gathered(weights[0, 0])
    first, second_shard, came_near, came, twin = lax.optimization_barrier(
        (first, weights[0, 1], came_near, came, twin)
    )
    second = gathered(second_shard)
    near = [jnp.where(decoder, mine, other) for mine, other in zip(own, came_near)]
    near[3] = near[3].reshape(micro_count, seq_length, 1)
    own = (*own[:3], own[3].reshape(micro_count, seq_length, 1))

    first_rows = first.reshape(8 * shard_rows, local_width)
    far = [
        lax.ppermute(partial, BOTH, DEC_SWAP)
        for partial in far_partial(core[None], came, twin, first_rows)
    ]
    own_partial = near_partial(half[None], grads, first_rows)
    ctx, ctx_near, ctx_own = [], [], []
    for micro in micros:
        part = far[micro]
        if micro > 0:
            part, ctx[-1] = lax.optimization_barrier((part, ctx[-1]))
        ctx.append((own_partial[micro] + part.astype(F32)).astype(BF16))
        ctx_near.append(lax.ppermute(ctx[micro], BOTH, DEC_TO_ENC))
        ctx_own.append(lax.ppermute(ctx_near[micro], BOTH, ENC_SWAP))

    near_flags = jnp.stack([dec, 1 - dec, dec])
    own_flags = jnp.stack([0 * dec, 1 - dec, 0 * dec])

    def attended(flags, held, sent, operands):
        grads = []
        for micro in micros:
            came = sent[micro]
            if micro > 0:
                came, grads[-1] = lax.optimization_barrier((came, grads[-1]))
            grads.append(attend(flags, held[micro], came, *operands, micro))
        return zip(*grads)

    dq, dk, dv = attended(near_flags, ctx, ctx_near, near)
    far_dq = []
    for micro in micros:
        far_dq.append(lax.ppermute(dq[micro], BOTH, DEC_SWAP))
    _, own_dk, own_dv = attended(own_flags, ctx, ctx_own, own)

    places = 2 * ((chip + jnp.array(STEPS, jnp.int32)) % 4)
    keep_at, give_at = places + core, places + 1 - core

    def chip_sums(grads):
        give = projected(give_at, dec[None], grads, first, second)
        other = lax.ppermute(give, "segment", CORE_SWAP)
        return projected(keep_at, dec[None], grads, first, second, other)

    def reduced(blocks, result):
        for step, block in zip(STEPS, blocks):
            pairs = [(2 * x + k, 2 * ((x + step) % 4) + k) for x in range(4) for k in range(2)]
            other = lax.ppermute(block, "segment", pairs)
            result = result + other.astype(F32)
        return result.astype(BF16)

    *blocks, block = chip_sums((*far_dq, *dk, *dv))
    own_grads, blocks = lax.optimization_barrier(((*dq, *own_dk, *own_dv), blocks))
    from_partner = lax.ppermute(reduced(blocks, block), "fsdp", HALF_SWAP)
    *blocks, block = chip_sums(own_grads)
    own_out = reduced(blocks, block)
    result = jnp.where(
        half == 0,
        jnp.concatenate([own_out, from_partner], axis=1),
        jnp.concatenate([from_partner, own_out], axis=1),
    )
    return result.reshape(1, micro_count, reaction_count, seq_length, 2 * shard_rows)


def solution(mesh):
    return jax.shard_map(
        per_device,
        mesh=mesh,
        in_specs=(
            P(None, "fsdp", None, None),
            P(None, "fsdp", None, "segment"),
            P(None, "fsdp", None, "segment"),
            P(None, "fsdp", None, "segment"),
            P(None, "fsdp", None),
            P("section", None, "fsdp", "segment"),
        ),
        out_specs=P("section", None, "fsdp", None, "segment"),
        check_vma=False,
    )
```

```python
import functools

import jax
import jax.numpy as jnp
from jax import lax
from jax.experimental import pallas as pl
from jax.experimental.pallas import tpu as pltpu
from jax.sharding import PartitionSpec as P


HDIM = 128

FAR_FIRST = (4, 3, 5, 2, 6, 1, 7)
DEC_SWAP = [(16 + f, 16 + (f ^ 1)) for f in range(16)]
ENC_SWAP = [(f, f ^ 1) for f in range(16)]
DEC_TO_ENC = [(16 + f, f ^ 1) for f in range(16)]
HALF_SWAP = [(f, f ^ 1) for f in range(16)]
CORE_SWAP = [(g, g ^ 1) for g in range(8)]
BOTH = ("section", "fsdp")
STEPS = (2, 1, 3, 0)
F32 = jnp.float32
SMALL = pltpu.CompilerParams(vmem_limit_bytes=20 * 2**20)
ANY = pl.BlockSpec(memory_space=pl.ANY)
BF16 = jnp.bfloat16
NT = (((1,), (1,)), ((), ()))
TN = (((0,), (0,)), ((), ()))
NN = (((1,), (0,)), ((), ()))


def mm(left, right, dims):
    return lax.dot_general(left, right, dims, preferred_element_type=F32)


def cost(flops, bytes_accessed):
    return pl.CostEstimate(flops=flops, bytes_accessed=bytes_accessed, transcendentals=0)


def pick_kernel(where, source, target):
    target[...] = source[...]


def picked(source, columns, width):
    rows = source.shape[0]
    count = columns.shape[0]
    return pl.pallas_call(
        pick_kernel,
        grid_spec=pltpu.PrefetchScalarGridSpec(
            num_scalar_prefetch=1,
            grid=(count,),
            in_specs=[pl.BlockSpec((rows, width), lambda i, at: (0, at[i]))],
            out_specs=pl.BlockSpec((rows, width), lambda i, at: (0, i)),
        ),
        out_shape=jax.ShapeDtypeStruct((rows, count * width), source.dtype),
        cost_estimate=cost(0, 2 * rows * count * width * 2),
        compiler_params=SMALL,
        name="pick",
    )(columns, source)


def fetched(step, weights, buffer, sems):
    rows = weights[0].shape[0]
    copies = [
        pltpu.make_async_copy(weight, buffer.at[pl.ds(d * rows, rows)], sems.at[d])
        for d, weight in enumerate(weights)
    ]

    @pl.when(step == 0)
    def _():
        for copy in copies:
            copy.start()

    for j in range(4):

        @pl.when(step == j)
        def _():
            copies[2 * j].wait()
            copies[2 * j + 1].wait()

    return buffer[pl.ds(pl.multiple_of(step * 2 * rows, 2 * rows), 2 * rows), :]


def added(step, acc, part):
    @pl.when(step == 0)
    def _():
        acc[...] = part

    @pl.when(step > 0)
    def _():
        acc[...] += part


def far_kernel(core, came, twin, *refs):
    weights, (low, high, acc, buffer, sems) = refs[:8], refs[8:]
    step = pl.program_id(0)
    rows = jnp.where(core[0] == step // 2, came[...], twin[...])
    added(step, acc, mm(rows, fetched(step, weights, buffer, sems), NN))

    @pl.when(step == pl.num_programs(0) - 1)
    def _():
        rows = low.shape[0]
        low[...] = acc[:rows].astype(BF16)
        high[...] = acc[rows:].astype(BF16)


def near_kernel(columns, first, second, *refs):
    weights, (low, high, buffer, sems) = refs[:8], refs[8:]
    step = pl.program_id(0)
    rows = jnp.concatenate([first[...], second[...]], axis=1)
    part = mm(rows, fetched(step, weights, buffer, sems), NN)
    half = low.shape[0]
    added(step, low, part[:half])
    added(step, high, part[half:])


def partial_products(scalars, operands, specs, weights, out_dtype, kernel):
    row_count = operands[0].shape[0]
    shard, width = weights[0].shape
    extra = [pltpu.VMEM((row_count, width), F32)] if out_dtype == BF16 else []
    return pl.pallas_call(
        kernel,
        grid_spec=pltpu.PrefetchScalarGridSpec(
            num_scalar_prefetch=1,
            grid=(4,),
            in_specs=specs + [ANY] * 8,
            out_specs=[pl.BlockSpec((row_count // 2, width), lambda j, at: (0, 0))] * 2,
            scratch_shapes=extra
            + [pltpu.VMEM((8 * shard, width), BF16), pltpu.SemaphoreType.DMA((8,))],
        ),
        out_shape=[jax.ShapeDtypeStruct((row_count // 2, width), out_dtype)] * 2,
        cost_estimate=cost(2 * row_count * 8 * shard * width, 2 * 8 * shard * width),
        compiler_params=SMALL,
    )(scalars, *operands, *weights)


def attend_kernel(heads, flags, *refs):
    *sent, query, key, value, mask, dq, dk, dv = refs if len(refs) > 8 else (*refs[:5], None, *refs[5:])
    scale = HDIM ** (-0.5)
    cuts = [slice(head * HDIM, (head + 1) * HDIM) for head in range(heads)]

    def grads_of(cut):
        grad = sent[0][:, cut]
        if len(sent) > 1:
            grad = jnp.where(flags[0] > 0, sent[1][:, cut], grad)
        q, k, v = query[:, cut], key[:, cut], value[:, cut]
        scores = jnp.where(mask[...] > 0, mm(k, q, NT) * scale, -jnp.inf)
        raised = jnp.exp(scores - jnp.max(scores, axis=0, keepdims=True))
        probs = raised * (1.0 / jnp.sum(raised, axis=0, keepdims=True))
        prob_grad = mm(v, grad, NT)
        center = jnp.sum(probs * prob_grad, axis=0, keepdims=True)
        return grad, q, k, probs, (probs * (prob_grad - center)).astype(BF16)

    def query_grads():
        for cut in cuts:
            _, _, k, _, score_grad = grads_of(cut)
            dq[:, cut] = (mm(score_grad, k, TN) * scale).astype(BF16)

    def key_value_grads():
        for cut in cuts:
            grad, q, _, probs, score_grad = grads_of(cut)
            dk[:, cut] = (mm(score_grad, q, NN) * scale).astype(BF16)
            dv[:, cut] = mm(probs.astype(BF16), grad, NN).astype(BF16)

    if len(sent) > 1:
        pl.when(flags[0] > 0)(query_grads)
    pl.when(flags[1] > 0)(key_value_grads)


def attend(flags, sent, query, key, value, mask, micro):
    seq_length, width = sent[0].shape
    heads = 2
    wide = heads * HDIM
    one = pl.BlockSpec((seq_length, wide), lambda h, flags: (0, h))
    row = pl.BlockSpec((None, seq_length, wide), lambda h, flags: (micro, 0, h))
    out = jax.ShapeDtypeStruct((seq_length, width), BF16)
    outs = 1 + len(sent)
    return pl.pallas_call(
        functools.partial(attend_kernel, heads),
        grid_spec=pltpu.PrefetchScalarGridSpec(
            num_scalar_prefetch=1,
            grid=(width // wide,),
            in_specs=[one] * len(sent)
            + [
                row,
                row,
                row,
                pl.BlockSpec((None, seq_length, 1), lambda h, flags: (micro, 0, 0)),
            ],
            out_specs=[one] * outs,
        ),
        out_shape=[out] * outs,
        cost_estimate=cost(
            10 * seq_length * seq_length * width, 16 * seq_length * width
        ),
        compiler_params=SMALL,
        name="attend",
    )(flags, *sent, query, key, value, mask)


def products(at, flags, refs):
    q0, q1, k0, k1, v0, v1 = refs[:6]
    weights = refs[6:14], refs[14:22]
    total, buffer, sems = refs[-3:]
    step = pl.program_id(0)

    def copy(which, place, d):
        return pltpu.make_async_copy(
            weights[which][d], buffer.at[which, place], sems.at[which, place]
        )

    @pl.when(step == 0)
    def _():
        for place in range(4):
            for d in range(8):

                @pl.when(at[place] == d)
                def _():
                    copy(1, place, d).start()

                    @pl.when(flags[0] == 0)
                    def _():
                        copy(0, place, d).start()

    copy(1, step, 0).wait()
    rows = jnp.where(
        flags[0] > 0,
        jnp.concatenate([q0[...], q1[...]]),
        jnp.concatenate([v0[...], v1[...]]),
    )
    total[...] = mm(rows, buffer[1, step], NT)

    @pl.when(flags[0] == 0)
    def _():
        copy(0, step, 0).wait()
        total[...] += mm(jnp.concatenate([k0[...], k1[...]]), buffer[0, step], NT)

    return total[...]


def give_kernel(at, flags, *refs):
    refs[22][...] = products(at, flags, refs).astype(BF16)


def keep_kernel(at, flags, *refs):
    other, outs = refs[22], refs[23:27]
    total = products(at, flags, refs) + other[...].astype(F32)
    for i, out in enumerate(outs):

        @pl.when(pl.program_id(0) == i)
        def _():
            out[...] = total.astype(out.dtype)


def projected(at, flags, grads, first, second, other=None):
    rows, width = grads[0].shape
    shard = first[0].shape[0]
    whole = pl.BlockSpec((rows, width), lambda i, at, flags: (0, 0))
    moving = pl.BlockSpec((None, 2 * rows, shard), lambda i, at, flags: (i, 0, 0))
    fixed = pl.BlockSpec((2 * rows, shard), lambda i, at, flags: (0, 0))
    if other is None:
        kernel, extra = give_kernel, ()
        out_specs = moving
        out_shape = jax.ShapeDtypeStruct((4, 2 * rows, shard), BF16)
    else:
        kernel, extra = keep_kernel, (other,)
        out_specs = [fixed] * 4
        out_shape = [jax.ShapeDtypeStruct((2 * rows, shard), t) for t in (BF16, BF16, BF16, F32)]
    return pl.pallas_call(
        kernel,
        grid_spec=pltpu.PrefetchScalarGridSpec(
            num_scalar_prefetch=2,
            grid=(4,),
            in_specs=[whole] * 6 + [ANY] * 16 + [moving] * len(extra),
            out_specs=out_specs,
            scratch_shapes=[
                pltpu.VMEM((2 * rows, shard), F32),
                pltpu.VMEM((2, 4, shard, width), BF16),
                pltpu.SemaphoreType.DMA((2, 4)),
            ],
        ),
        out_shape=out_shape,
        cost_estimate=cost(2 * 2 * rows * 2 * width * 4 * shard, 2 * 2 * 4 * shard * width),
        compiler_params=SMALL,
    )(at, flags, *grads, *first, *second, *extra)


def per_device(out_grad, queries, enc_keys, enc_values, key_mask, weights):
    decoder = lax.axis_index("section") == 1
    half = lax.axis_index("fsdp") % 2
    line = lax.axis_index("fsdp") // 2
    segment = lax.axis_index("segment")
    core = segment % 2
    chip = segment // 2
    micro_count, reaction_count, seq_length, feature_width = out_grad.shape
    local_width = queries.shape[3]
    shard_rows = weights.shape[2]
    row_count = micro_count * reaction_count * seq_length
    flat = (micro_count, seq_length, local_width)
    micros = range(micro_count)
    dec = decoder.astype(jnp.int32)

    def gathered(shard):
        found = {0: shard}
        for d in FAR_FIRST:
            pairs = [(f, (f + 2 * d) % 16) for f in range(16)]
            found[d] = lax.ppermute(shard, "fsdp", pairs)
        return [found[d] for d in range(8)]

    grads = out_grad.reshape(row_count, feature_width)
    sources = (line - jnp.arange(8, dtype=jnp.int32)) % 8
    columns = 2 * ((line - 4 * core - jnp.arange(4, dtype=jnp.int32)) % 8) + 1 - half
    came = lax.ppermute(picked(grads, columns, shard_rows), BOTH, DEC_SWAP)
    twin = lax.ppermute(came, "segment", CORE_SWAP)

    own = (
        queries.reshape(flat),
        enc_keys.reshape(flat),
        enc_values.reshape(flat),
        key_mask.reshape(micro_count, 1, seq_length),
    )
    came_near = []
    for value in own:
        came_near.append(lax.ppermute(value, BOTH, ENC_SWAP))

    first = gathered(weights[0, 0])
    second_shard, *first[3:6] = lax.optimization_barrier((weights[0, 1], *first[3:6]))
    second = gathered(second_shard)
    near = [jnp.where(decoder, mine, other) for mine, other in zip(own, came_near)]
    near[3] = near[3].reshape(micro_count, seq_length, 1)
    own = (*own[:3], own[3].reshape(micro_count, seq_length, 1))

    piece = 2 * shard_rows
    moved = pl.BlockSpec((row_count, piece), lambda j, at: (0, j % 2))
    far = []
    for partial in partial_products(core[None], (came, twin), [moved] * 2, first, BF16, far_kernel):
        far.append(lax.ppermute(partial, BOTH, DEC_SWAP))
    own_partial = partial_products(
        2 * sources + half,
        (grads, grads),
        [
            pl.BlockSpec((row_count, shard_rows), lambda j, at: (0, at[2 * j])),
            pl.BlockSpec((row_count, shard_rows), lambda j, at: (0, at[2 * j + 1])),
        ],
        first,
        F32,
        near_kernel,
    )
    ctx, ctx_near, ctx_own = [], [], []
    for micro in micros:
        part = far[micro]
        if micro > 0:
            part, ctx[-1] = lax.optimization_barrier((part, ctx[-1]))
        ctx.append((own_partial[micro] + part.astype(F32)).astype(BF16))
        ctx_near.append(lax.ppermute(ctx[micro], BOTH, DEC_TO_ENC))
        ctx_own.append(lax.ppermute(ctx_near[micro], BOTH, ENC_SWAP))

    near_flags = jnp.stack([dec, 1 - dec])
    own_flags = jnp.stack([0 * dec, 1 - dec])

    def attended(flags, sent, held, operands):
        grads = []
        for micro in micros:
            came = sent[micro]
            if micro > 0:
                came, grads[-1] = lax.optimization_barrier((came, grads[-1]))
            grads.append(attend(flags, (came, *held[micro : micro + 1]), *operands, micro))
        return zip(*grads)

    dq, dk, dv = attended(near_flags, ctx_near, ctx, near)
    far_dq = []
    for micro in micros:
        far_dq.append(lax.ppermute(dq[micro], BOTH, DEC_SWAP))
    own_dk, own_dv = attended(own_flags, ctx_own, (), own)

    places = 2 * ((chip + jnp.array(STEPS, jnp.int32)) % 4)
    keep_at, give_at = (line - places - core) % 8, (line - places - 1 + core) % 8

    def chip_sums(grads):
        give = projected(give_at, dec[None], grads, first, second)
        other = lax.ppermute(give, "segment", CORE_SWAP)
        return projected(keep_at, dec[None], grads, first, second, other)

    def reduced(blocks, result):
        for step, block in zip(STEPS, blocks):
            pairs = [(2 * x + k, 2 * ((x + step) % 4) + k) for x in range(4) for k in range(2)]
            other = lax.ppermute(block, "segment", pairs)
            result = result + other.astype(F32)
        return result.astype(BF16)

    *blocks, block = chip_sums((*far_dq, *dk, *dv))
    own_grads, blocks = lax.optimization_barrier(((*dq, *own_dk, *own_dv), blocks))
    from_partner = lax.ppermute(reduced(blocks, block), "fsdp", HALF_SWAP)
    *blocks, block = chip_sums(own_grads)
    own_out = reduced(blocks, block)
    result = jnp.where(
        half == 0,
        jnp.concatenate([own_out, from_partner], axis=1),
        jnp.concatenate([from_partner, own_out], axis=1),
    )
    return result.reshape(1, micro_count, reaction_count, seq_length, 2 * shard_rows)


def solution(mesh):
    return jax.shard_map(
        per_device,
        mesh=mesh,
        in_specs=(
            P(None, "fsdp", None, None),
            P(None, "fsdp", None, "segment"),
            P(None, "fsdp", None, "segment"),
            P(None, "fsdp", None, "segment"),
            P(None, "fsdp", None),
            P("section", None, "fsdp", "segment"),
        ),
        out_specs=P("section", None, "fsdp", None, "segment"),
        check_vma=False,
    )
```

```python
import functools

import jax
import jax.numpy as jnp
from jax import lax
from jax.experimental import pallas as pl
from jax.experimental.pallas import tpu as pltpu
from jax.sharding import PartitionSpec as P


HDIM = 128

Z_LINES = [[2 * z + half for z in range(8)] for half in range(2)]
DEC_SWAP = [(16 + f, 16 + (f ^ 1)) for f in range(16)]
ENC_SWAP = [(f, f ^ 1) for f in range(16)]
DEC_TO_ENC = [(16 + f, f ^ 1) for f in range(16)]
HALF_SWAP = [(f, f ^ 1) for f in range(16)]
CORE_SWAP = [(g, g ^ 1) for g in range(8)]
BOTH = ("section", "fsdp")
STEPS = (2, 1, 3, 0)
F32 = jnp.float32
HBM = pl.BlockSpec(memory_space=pltpu.HBM)
BF16 = jnp.bfloat16
NT = (((1,), (1,)), ((), ()))
TN = (((0,), (0,)), ((), ()))
NN = (((1,), (0,)), ((), ()))


def mm(left, right, dims):
    return lax.dot_general(left, right, dims, preferred_element_type=F32)


def cost(flops, bytes_accessed):
    return pl.CostEstimate(flops=flops, bytes_accessed=bytes_accessed, transcendentals=0)


def pick_kernel(where, source, target):
    target[...] = source[...]


def picked(source, columns, width):
    rows = source.shape[0]
    count = columns.shape[0]
    return pl.pallas_call(
        pick_kernel,
        grid_spec=pltpu.PrefetchScalarGridSpec(
            num_scalar_prefetch=1,
            grid=(count,),
            in_specs=[pl.BlockSpec((rows, width), lambda i, at: (0, at[i]))],
            out_specs=pl.BlockSpec((rows, width), lambda i, at: (0, i)),
        ),
        out_shape=jax.ShapeDtypeStruct((rows, count * width), source.dtype),
        cost_estimate=cost(0, 2 * rows * count * width * 2),
        name="pick",
    )(columns, source)


def fetched(step, weight, buffer, sems):
    rows = weight.shape[1]
    copies = [
        pltpu.make_async_copy(weight.at[z], buffer.at[pl.ds(z * rows, rows)], sems.at[z])
        for z in range(8)
    ]

    @pl.when(step == 0)
    def _():
        for copy in copies:
            copy.start()

    for j in range(4):

        @pl.when(step == j)
        def _():
            copies[2 * j].wait()
            copies[2 * j + 1].wait()

    return buffer[pl.ds(pl.multiple_of(step * 2 * rows, 2 * rows), 2 * rows), :]


def added(step, acc, part):
    @pl.when(step == 0)
    def _():
        acc[...] = part

    @pl.when(step > 0)
    def _():
        acc[...] += part


def far_kernel(core, came, twin, weight, low, high, acc, buffer, sems):
    step = pl.program_id(0)
    rows = jnp.where(core[0] == step // 2, came[...], twin[...])
    added(step, acc, mm(rows, fetched(step, weight, buffer, sems), NN))

    @pl.when(step == pl.num_programs(0) - 1)
    def _():
        rows = low.shape[0]
        low[...] = acc[:rows].astype(BF16)
        high[...] = acc[rows:].astype(BF16)


def near_kernel(half, first, second, weight, low, high, buffer, sems):
    step = pl.program_id(0)
    rows = jnp.concatenate([first[...], second[...]], axis=1)
    part = mm(rows, fetched(step, weight, buffer, sems), NN)
    count = low.shape[0]
    added(step, low, part[:count])
    added(step, high, part[count:])


def partial_products(scalars, operands, specs, weight, out_dtype, kernel):
    row_count = operands[0].shape[0]
    _, shard, width = weight.shape
    extra = [pltpu.VMEM((row_count, width), F32)] if out_dtype == BF16 else []
    return pl.pallas_call(
        kernel,
        grid_spec=pltpu.PrefetchScalarGridSpec(
            num_scalar_prefetch=1,
            grid=(4,),
            in_specs=specs + [HBM],
            out_specs=[pl.BlockSpec((row_count // 2, width), lambda j, at: (0, 0))] * 2,
            scratch_shapes=extra
            + [pltpu.VMEM((8 * shard, width), BF16), pltpu.SemaphoreType.DMA((8,))],
        ),
        out_shape=[jax.ShapeDtypeStruct((row_count // 2, width), out_dtype)] * 2,
        cost_estimate=cost(2 * row_count * 8 * shard * width, 2 * 8 * shard * width),
    )(scalars, *operands, weight)


def attend_kernel(heads, flags, *refs):
    *sent, query, key, value, mask, dq, dk, dv = refs if len(refs) > 8 else (*refs[:5], None, *refs[5:])
    scale = HDIM ** (-0.5)
    cuts = [slice(head * HDIM, (head + 1) * HDIM) for head in range(heads)]

    def grads_of(cut):
        grad = sent[0][:, cut]
        if len(sent) > 1:
            grad = jnp.where(flags[0] > 0, sent[1][:, cut], grad)
        q, k, v = query[:, cut], key[:, cut], value[:, cut]
        scores = jnp.where(mask[...] > 0, mm(k, q, NT) * scale, -jnp.inf)
        raised = jnp.exp(scores - jnp.max(scores, axis=0, keepdims=True))
        probs = raised * (1.0 / jnp.sum(raised, axis=0, keepdims=True))
        prob_grad = mm(v, grad, NT)
        center = jnp.sum(probs * prob_grad, axis=0, keepdims=True)
        return grad, q, k, probs, (probs * (prob_grad - center)).astype(BF16)

    def query_grads():
        for cut in cuts:
            _, _, k, _, score_grad = grads_of(cut)
            dq[:, cut] = (mm(score_grad, k, TN) * scale).astype(BF16)

    def key_value_grads():
        for cut in cuts:
            grad, q, _, probs, score_grad = grads_of(cut)
            dk[:, cut] = (mm(score_grad, q, NN) * scale).astype(BF16)
            dv[:, cut] = mm(probs.astype(BF16), grad, NN).astype(BF16)

    if len(sent) > 1:
        pl.when(flags[0] > 0)(query_grads)
    pl.when(flags[1] > 0)(key_value_grads)


def attend(flags, sent, query, key, value, mask, micro):
    seq_length, width = sent[0].shape
    heads = 2
    wide = heads * HDIM
    one = pl.BlockSpec((seq_length, wide), lambda h, flags: (0, h))
    row = pl.BlockSpec((None, seq_length, wide), lambda h, flags: (micro, 0, h))
    out = jax.ShapeDtypeStruct((seq_length, width), BF16)
    outs = 1 + len(sent)
    return pl.pallas_call(
        functools.partial(attend_kernel, heads),
        grid_spec=pltpu.PrefetchScalarGridSpec(
            num_scalar_prefetch=1,
            grid=(width // wide,),
            in_specs=[one] * len(sent)
            + [
                row,
                row,
                row,
                pl.BlockSpec((None, seq_length, 1), lambda h, flags: (micro, 0, 0)),
            ],
            out_specs=[one] * outs,
        ),
        out_shape=[out] * outs,
        cost_estimate=cost(
            10 * seq_length * seq_length * width, 16 * seq_length * width
        ),
        name="attend",
    )(flags, *sent, query, key, value, mask)


def products(at, flags, refs):
    q0, q1, k0, k1, v0, v1 = refs[:6]
    weights = refs[6:8]
    buffer, sems = refs[-2:]
    step = pl.program_id(0)
    encoder = flags[0] == 0

    def copy(which, place):
        return pltpu.make_async_copy(
            weights[which].at[at[place]], buffer.at[which, place], sems.at[which, place]
        )

    def wide(which):
        pair = buffer[which, pl.ds(2 * step, 2)]
        return pair.reshape(pair.shape[0] * pair.shape[1], pair.shape[2])

    @pl.when(step == 0)
    def _():
        for place in range(4):
            copy(1, place).start()

            @pl.when(encoder)
            def _():
                copy(0, place).start()

    for place in range(2):
        copy(1, 2 * step + place).wait()

        @pl.when(encoder)
        def _():
            copy(0, 2 * step + place).wait()

    return (q0, q1), (k0, k1), (v0, v1), wide, encoder


def whole(pair):
    return jnp.concatenate([x[...] for x in pair])


def give_kernel(at, flags, *refs):
    out, total = refs[8], refs[-3]
    dq, dk, dv, wide, encoder = products(at, flags, refs)
    rows = jnp.where(encoder, whole(dv), whole(dq))
    total[...] = mm(rows, wide(1), NT)

    @pl.when(encoder)
    def _():
        total[...] += mm(whole(dk), wide(0), NT)

    shard = out.shape[2]
    for place in range(2):
        out[place] = total[:, place * shard : (place + 1) * shard].astype(BF16)


def keep_kernel(at, flags, *refs):
    other, outs, total = refs[8], refs[9:13], refs[-3]
    dq, dk, dv, wide, encoder = products(at, flags, refs)
    rows = jnp.where(encoder, whole(dv), whole(dq))
    total[...] = mm(rows, wide(1), NT)

    @pl.when(encoder)
    def _():
        total[...] += mm(whole(dk), wide(0), NT)

    shard = outs[0].shape[1]
    for i, out in enumerate(outs):

        @pl.when(pl.program_id(0) == i // 2)
        def _():
            cut = slice(i % 2 * shard, (i % 2 + 1) * shard)
            out[...] = (total[:, cut] + other[i % 2].astype(F32)).astype(out.dtype)


def projected(at, flags, grads, first, second, other=None):
    rows, width = grads[0].shape
    shard = first.shape[1]
    operand = pl.BlockSpec((rows, width), lambda i, at, flags: (0, 0))
    moving = pl.BlockSpec((2, 2 * rows, shard), lambda i, at, flags: (i, 0, 0))
    fixed = pl.BlockSpec((2 * rows, shard), lambda i, at, flags: (0, 0))
    if other is None:
        kernel, extra = give_kernel, ()
        out_specs = moving
        out_shape = jax.ShapeDtypeStruct((4, 2 * rows, shard), BF16)
    else:
        kernel, extra = keep_kernel, (other,)
        out_specs = [fixed] * 4
        out_shape = [jax.ShapeDtypeStruct((2 * rows, shard), t) for t in (BF16, BF16, BF16, F32)]
    return pl.pallas_call(
        kernel,
        grid_spec=pltpu.PrefetchScalarGridSpec(
            num_scalar_prefetch=2,
            grid=(2,),
            in_specs=[operand] * 6 + [HBM] * 2 + [moving] * len(extra),
            out_specs=out_specs,
            scratch_shapes=[
                pltpu.VMEM((2 * rows, 2 * shard), F32),
                pltpu.VMEM((2, 4, shard, width), BF16),
                pltpu.SemaphoreType.DMA((2, 4)),
            ],
        ),
        out_shape=out_shape,
        cost_estimate=cost(2 * 2 * rows * 2 * width * 4 * shard, 2 * 2 * 4 * shard * width),
    )(at, flags, *grads, first, second, *extra)


def per_device(out_grad, queries, enc_keys, enc_values, key_mask, weights):
    decoder = lax.axis_index("section") == 1
    half = lax.axis_index("fsdp") % 2
    segment = lax.axis_index("segment")
    core = segment % 2
    chip = segment // 2
    micro_count, reaction_count, seq_length, feature_width = out_grad.shape
    local_width = queries.shape[3]
    shard_rows = weights.shape[2]
    row_count = micro_count * reaction_count * seq_length
    flat = (micro_count, seq_length, local_width)
    micros = range(micro_count)
    dec = decoder.astype(jnp.int32)

    def gathered(shard):
        return lax.all_gather(shard, "fsdp", axis=0, axis_index_groups=Z_LINES)

    grads = out_grad.reshape(row_count, feature_width)
    columns = 2 * (4 * core + jnp.arange(4, dtype=jnp.int32)) + 1 - half
    came = lax.ppermute(picked(grads, columns, shard_rows), BOTH, DEC_SWAP)
    twin = lax.ppermute(came, "segment", CORE_SWAP)

    own = (
        queries.reshape(flat),
        enc_keys.reshape(flat),
        enc_values.reshape(flat),
        key_mask.reshape(micro_count, 1, seq_length),
    )
    came_near = []
    for value in own:
        came_near.append(lax.ppermute(value, BOTH, ENC_SWAP))

    first = gathered(weights[0, 0])
    first, second_shard, came, twin = lax.optimization_barrier(
        (first, weights[0, 1], came, twin)
    )
    second = gathered(second_shard)
    near = [jnp.where(decoder, mine, other) for mine, other in zip(own, came_near)]
    near[3] = near[3].reshape(micro_count, seq_length, 1)
    own = (*own[:3], own[3].reshape(micro_count, seq_length, 1))

    piece = 2 * shard_rows
    moved = pl.BlockSpec((row_count, piece), lambda j, at: (0, j % 2))
    far = []
    for partial in partial_products(core[None], (came, twin), [moved] * 2, first, BF16, far_kernel):
        far.append(lax.ppermute(partial, BOTH, DEC_SWAP))
    own_partial = partial_products(
        half[None],
        (grads, grads),
        [
            pl.BlockSpec((row_count, shard_rows), lambda j, half: (0, 4 * j + half[0])),
            pl.BlockSpec((row_count, shard_rows), lambda j, half: (0, 4 * j + 2 + half[0])),
        ],
        first,
        F32,
        near_kernel,
    )
    ctx, ctx_near, ctx_own = [], [], []
    for micro in micros:
        part = far[micro]
        if micro > 0:
            part, ctx[-1] = lax.optimization_barrier((part, ctx[-1]))
        ctx.append((own_partial[micro] + part.astype(F32)).astype(BF16))
        ctx_near.append(lax.ppermute(ctx[micro], BOTH, DEC_TO_ENC))
        ctx_own.append(lax.ppermute(ctx_near[micro], BOTH, ENC_SWAP))

    near_flags = jnp.stack([dec, 1 - dec])
    own_flags = jnp.stack([0 * dec, 1 - dec])

    def attended(flags, sent, held, operands):
        grads = []
        for micro in micros:
            came = sent[micro]
            if micro > 0:
                came, grads[-1] = lax.optimization_barrier((came, grads[-1]))
            grads.append(attend(flags, (came, *held[micro : micro + 1]), *operands, micro))
        return zip(*grads)

    dq, dk, dv = attended(near_flags, ctx_near, ctx, near)
    far_dq = []
    for micro in micros:
        far_dq.append(lax.ppermute(dq[micro], BOTH, DEC_SWAP))
    own_dk, own_dv = attended(own_flags, ctx_own, (), own)

    places = 2 * ((chip + jnp.array(STEPS, jnp.int32)) % 4)
    keep_at, give_at = places + core, places + 1 - core

    def chip_sums(grads):
        give = projected(give_at, dec[None], grads, first, second)
        other = lax.ppermute(give, "segment", CORE_SWAP)
        return projected(keep_at, dec[None], grads, first, second, other)

    def reduced(blocks, result):
        for step, block in zip(STEPS, blocks):
            pairs = [(2 * x + k, 2 * ((x + step) % 4) + k) for x in range(4) for k in range(2)]
            other = lax.ppermute(block, "segment", pairs)
            result = result + other.astype(F32)
        return result.astype(BF16)

    *blocks, block = chip_sums((*far_dq, *dk, *dv))
    own_grads, blocks = lax.optimization_barrier(((*dq, *own_dk, *own_dv), blocks))
    from_partner = lax.ppermute(reduced(blocks, block), "fsdp", HALF_SWAP)
    *blocks, block = chip_sums(own_grads)
    own_out = reduced(blocks, block)
    result = jnp.where(
        half == 0,
        jnp.concatenate([own_out, from_partner], axis=1),
        jnp.concatenate([from_partner, own_out], axis=1),
    )
    return result.reshape(1, micro_count, reaction_count, seq_length, 2 * shard_rows)


def solution(mesh):
    return jax.shard_map(
        per_device,
        mesh=mesh,
        in_specs=(
            P(None, "fsdp", None, None),
            P(None, "fsdp", None, "segment"),
            P(None, "fsdp", None, "segment"),
            P(None, "fsdp", None, "segment"),
            P(None, "fsdp", None),
            P("section", None, "fsdp", "segment"),
        ),
        out_specs=P("section", None, "fsdp", None, "segment"),
        check_vma=False,
    )
```

```python
import functools

import jax
import jax.numpy as jnp
from jax import lax
from jax.experimental import pallas as pl
from jax.experimental.pallas import tpu as pltpu
from jax.sharding import PartitionSpec as P


HDIM = 128

Z_LINES = [[2 * z + half for z in range(8)] for half in range(2)]
DEC_SWAP = [(16 + f, 16 + (f ^ 1)) for f in range(16)]
ENC_SWAP = [(f, f ^ 1) for f in range(16)]
DEC_TO_ENC = [(16 + f, f ^ 1) for f in range(16)]
HALF_SWAP = [(f, f ^ 1) for f in range(16)]
CORE_SWAP = [(g, g ^ 1) for g in range(8)]
BOTH = ("section", "fsdp")
STEPS = (2, 1, 3, 0)
F32 = jnp.float32
HBM = pl.BlockSpec(memory_space=pltpu.HBM)
BF16 = jnp.bfloat16
NT = (((1,), (1,)), ((), ()))
TN = (((0,), (0,)), ((), ()))
NN = (((1,), (0,)), ((), ()))


def mm(left, right, dims):
    return lax.dot_general(left, right, dims, preferred_element_type=F32)


def cost(flops, bytes_accessed):
    return pl.CostEstimate(flops=flops, bytes_accessed=bytes_accessed, transcendentals=0)


def pick_kernel(where, source, target):
    target[...] = source[...]


def picked(source, columns, width):
    rows = source.shape[0]
    count = columns.shape[0]
    return pl.pallas_call(
        pick_kernel,
        grid_spec=pltpu.PrefetchScalarGridSpec(
            num_scalar_prefetch=1,
            grid=(count,),
            in_specs=[pl.BlockSpec((rows, width), lambda i, at: (0, at[i]))],
            out_specs=pl.BlockSpec((rows, width), lambda i, at: (0, i)),
        ),
        out_shape=jax.ShapeDtypeStruct((rows, count * width), source.dtype),
        cost_estimate=cost(0, 2 * rows * count * width * 2),
        name="pick",
    )(columns, source)


def fetched(step, weight, buffer, sems):
    rows = weight.shape[1]
    copies = [
        pltpu.make_async_copy(weight.at[z], buffer.at[pl.ds(z * rows, rows)], sems.at[z])
        for z in range(8)
    ]

    @pl.when(step == 0)
    def _():
        for copy in copies:
            copy.start()

    for j in range(4):

        @pl.when(step == j)
        def _():
            copies[2 * j].wait()
            copies[2 * j + 1].wait()

    return buffer[pl.ds(pl.multiple_of(step * 2 * rows, 2 * rows), 2 * rows), :]


def added(step, acc, part):
    @pl.when(step == 0)
    def _():
        acc[...] = part

    @pl.when(step > 0)
    def _():
        acc[...] += part


def far_kernel(core, came, twin, weight, low, high, acc, buffer, sems):
    step = pl.program_id(0)
    rows = jnp.where(core[0] == step // 2, came[...], twin[...])
    added(step, acc, mm(rows, fetched(step, weight, buffer, sems), NN))

    @pl.when(step == pl.num_programs(0) - 1)
    def _():
        rows = low.shape[0]
        low[...] = acc[:rows].astype(BF16)
        high[...] = acc[rows:].astype(BF16)


def near_kernel(half, first, second, weight, low, high, buffer, sems):
    step = pl.program_id(0)
    rows = jnp.concatenate([first[...], second[...]], axis=1)
    part = mm(rows, fetched(step, weight, buffer, sems), NN)
    count = low.shape[0]
    added(step, low, part[:count])
    added(step, high, part[count:])


def partial_products(scalars, operands, specs, weight, out_dtype, kernel):
    row_count = operands[0].shape[0]
    _, shard, width = weight.shape
    extra = [pltpu.VMEM((row_count, width), F32)] if out_dtype == BF16 else []
    return pl.pallas_call(
        kernel,
        grid_spec=pltpu.PrefetchScalarGridSpec(
            num_scalar_prefetch=1,
            grid=(4,),
            in_specs=specs + [HBM],
            out_specs=[pl.BlockSpec((row_count // 2, width), lambda j, at: (0, 0))] * 2,
            scratch_shapes=extra
            + [pltpu.VMEM((8 * shard, width), BF16), pltpu.SemaphoreType.DMA((8,))],
        ),
        out_shape=[jax.ShapeDtypeStruct((row_count // 2, width), out_dtype)] * 2,
        cost_estimate=cost(2 * row_count * 8 * shard * width, 2 * 8 * shard * width),
    )(scalars, *operands, weight)


def attend_kernel(heads, flags, *refs):
    *sent, query, key, value, mask, dq, dk, dv = refs if len(refs) > 8 else (*refs[:5], None, *refs[5:])
    scale = HDIM ** (-0.5)
    cuts = [slice(head * HDIM, (head + 1) * HDIM) for head in range(heads)]

    def grads_of(cut):
        grad = sent[0][:, cut]
        if len(sent) > 1:
            grad = jnp.where(flags[0] > 0, sent[1][:, cut], grad)
        q, k, v = query[:, cut], key[:, cut], value[:, cut]
        scores = jnp.where(mask[:, :1] > 0, mm(k, q, NT) * scale, -jnp.inf)
        raised = jnp.exp(scores - jnp.max(scores, axis=0, keepdims=True))
        probs = raised * (1.0 / jnp.sum(raised, axis=0, keepdims=True))
        prob_grad = mm(v, grad, NT)
        center = jnp.sum(probs * prob_grad, axis=0, keepdims=True)
        return grad, q, k, probs, (probs * (prob_grad - center)).astype(BF16)

    def query_grads():
        for cut in cuts:
            _, _, k, _, score_grad = grads_of(cut)
            dq[:, cut] = (mm(score_grad, k, TN) * scale).astype(BF16)

    def key_value_grads():
        for cut in cuts:
            grad, q, _, probs, score_grad = grads_of(cut)
            dk[:, cut] = (mm(score_grad, q, NN) * scale).astype(BF16)
            dv[:, cut] = mm(probs.astype(BF16), grad, NN).astype(BF16)

    if len(sent) > 1:
        pl.when(flags[0] > 0)(query_grads)
    pl.when(flags[1] > 0)(key_value_grads)


def attend(flags, sent, query, key, value, mask, micro):
    seq_length, width = sent[0].shape
    heads = 2
    wide = heads * HDIM
    one = pl.BlockSpec((seq_length, wide), lambda h, flags: (0, h))
    row = pl.BlockSpec((None, seq_length, wide), lambda h, flags: (micro, 0, h))
    out = jax.ShapeDtypeStruct((seq_length, width), BF16)
    outs = 1 + len(sent)
    return pl.pallas_call(
        functools.partial(attend_kernel, heads),
        grid_spec=pltpu.PrefetchScalarGridSpec(
            num_scalar_prefetch=1,
            grid=(width // wide,),
            in_specs=[one] * len(sent)
            + [
                row,
                row,
                row,
                pl.BlockSpec((None, seq_length, HDIM), lambda h, flags: (micro, 0, 0)),
            ],
            out_specs=[one] * outs,
        ),
        out_shape=[out] * outs,
        cost_estimate=cost(
            10 * seq_length * seq_length * width, 16 * seq_length * width
        ),
        name="attend",
    )(flags, *sent, query, key, value, mask)


def products(at, flags, refs):
    q0, q1, k0, k1, v0, v1 = refs[:6]
    weights = refs[6:8]
    buffer, sems = refs[-2:]
    step = pl.program_id(0)
    encoder = flags[0] == 0

    def copy(which, place):
        return pltpu.make_async_copy(
            weights[which].at[at[place]], buffer.at[which, place], sems.at[which, place]
        )

    def wide(which):
        pair = buffer[which, pl.ds(2 * step, 2)]
        return pair.reshape(pair.shape[0] * pair.shape[1], pair.shape[2])

    @pl.when(step == 0)
    def _():
        for place in range(4):
            copy(1, place).start()

            @pl.when(encoder)
            def _():
                copy(0, place).start()

    for place in range(2):
        copy(1, 2 * step + place).wait()

        @pl.when(encoder)
        def _():
            copy(0, 2 * step + place).wait()

    return (q0, q1), (k0, k1), (v0, v1), wide, encoder


def whole(pair):
    return jnp.concatenate([x[...] for x in pair])


def give_kernel(at, flags, *refs):
    out, total = refs[8], refs[-3]
    dq, dk, dv, wide, encoder = products(at, flags, refs)
    rows = jnp.where(encoder, whole(dv), whole(dq))
    total[...] = mm(rows, wide(1), NT)

    @pl.when(encoder)
    def _():
        total[...] += mm(whole(dk), wide(0), NT)

    shard = out.shape[2]
    for place in range(2):
        out[place] = total[:, place * shard : (place + 1) * shard].astype(BF16)


def keep_kernel(at, flags, *refs):
    other, outs, total = refs[8], refs[9:13], refs[-3]
    dq, dk, dv, wide, encoder = products(at, flags, refs)
    rows = jnp.where(encoder, whole(dv), whole(dq))
    total[...] = mm(rows, wide(1), NT)

    @pl.when(encoder)
    def _():
        total[...] += mm(whole(dk), wide(0), NT)

    shard = outs[0].shape[1]
    for i, out in enumerate(outs):

        @pl.when(pl.program_id(0) == i // 2)
        def _():
            cut = slice(i % 2 * shard, (i % 2 + 1) * shard)
            out[...] = (total[:, cut] + other[i % 2].astype(F32)).astype(out.dtype)


def projected(at, flags, grads, first, second, other=None):
    rows, width = grads[0].shape
    shard = first.shape[1]
    operand = pl.BlockSpec((rows, width), lambda i, at, flags: (0, 0))
    moving = pl.BlockSpec((2, 2 * rows, shard), lambda i, at, flags: (i, 0, 0))
    fixed = pl.BlockSpec((2 * rows, shard), lambda i, at, flags: (0, 0))
    if other is None:
        kernel, extra = give_kernel, ()
        out_specs = moving
        out_shape = jax.ShapeDtypeStruct((4, 2 * rows, shard), BF16)
    else:
        kernel, extra = keep_kernel, (other,)
        out_specs = [fixed] * 4
        out_shape = [jax.ShapeDtypeStruct((2 * rows, shard), t) for t in (BF16, BF16, BF16, F32)]
    return pl.pallas_call(
        kernel,
        grid_spec=pltpu.PrefetchScalarGridSpec(
            num_scalar_prefetch=2,
            grid=(2,),
            in_specs=[operand] * 6 + [HBM] * 2 + [moving] * len(extra),
            out_specs=out_specs,
            scratch_shapes=[
                pltpu.VMEM((2 * rows, 2 * shard), F32),
                pltpu.VMEM((2, 4, shard, width), BF16),
                pltpu.SemaphoreType.DMA((2, 4)),
            ],
        ),
        out_shape=out_shape,
        cost_estimate=cost(2 * 2 * rows * 2 * width * 4 * shard, 2 * 2 * 4 * shard * width),
    )(at, flags, *grads, first, second, *extra)


def per_device(out_grad, queries, enc_keys, enc_values, key_mask, weights):
    decoder = lax.axis_index("section") == 1
    half = lax.axis_index("fsdp") % 2
    segment = lax.axis_index("segment")
    core = segment % 2
    chip = segment // 2
    micro_count, reaction_count, seq_length, feature_width = out_grad.shape
    local_width = queries.shape[3]
    shard_rows = weights.shape[2]
    row_count = micro_count * reaction_count * seq_length
    flat = (micro_count, seq_length, local_width)
    micros = range(micro_count)
    dec = decoder.astype(jnp.int32)

    def gathered(shard):
        return lax.all_gather(shard, "fsdp", axis=0, axis_index_groups=Z_LINES)

    own = (
        queries.reshape(flat),
        enc_keys.reshape(flat),
        enc_values.reshape(flat),
        key_mask.reshape(micro_count, 1, seq_length),
    )
    came_near = []
    for value in own:
        came_near.append(lax.ppermute(value, BOTH, ENC_SWAP))
    near = [jnp.where(decoder, mine, other) for mine, other in zip(own, came_near)]
    near[3], own_mask = [
        jnp.broadcast_to(mask.reshape(micro_count, seq_length, 1), (micro_count, seq_length, HDIM))
        for mask in (near[3], own[3])
    ]

    near_flags = jnp.stack([dec, 1 - dec])
    own_flags = jnp.stack([0 * dec, 1 - dec])
    places = 2 * ((chip + jnp.array(STEPS, jnp.int32)) % 4)
    keep_at, give_at = places + core, places + 1 - core

    grads = out_grad.reshape(row_count, feature_width)
    columns = 2 * (4 * core + jnp.arange(4, dtype=jnp.int32)) + 1 - half
    first = gathered(weights[0, 0])
    part = picked(grads, columns, shard_rows)
    part, later_weights = lax.optimization_barrier((part, weights))
    came = lax.ppermute(part, BOTH, DEC_SWAP)
    twin = lax.ppermute(came, "segment", CORE_SWAP)

    ready = (came, twin, later_weights[0, 1], near, own_mask, near_flags, own_flags, keep_at, give_at)
    first, ready = lax.optimization_barrier((first, ready))
    came, twin, second_shard, near, own_mask, near_flags, own_flags, keep_at, give_at = ready
    own = (*own[:3], own_mask)
    second = gathered(second_shard)

    piece = 2 * shard_rows
    moved = pl.BlockSpec((row_count, piece), lambda j, at: (0, j % 2))
    far = []
    for partial in partial_products(core[None], (came, twin), [moved] * 2, first, BF16, far_kernel):
        far.append(lax.ppermute(partial, BOTH, DEC_SWAP))
    own_partial = partial_products(
        half[None],
        (grads, grads),
        [
            pl.BlockSpec((row_count, shard_rows), lambda j, half: (0, 4 * j + half[0])),
            pl.BlockSpec((row_count, shard_rows), lambda j, half: (0, 4 * j + 2 + half[0])),
        ],
        first,
        F32,
        near_kernel,
    )
    ctx, ctx_near, ctx_own = [], [], []
    for micro in micros:
        part = far[micro]
        if micro > 0:
            part, ctx[-1] = lax.optimization_barrier((part, ctx[-1]))
        ctx.append((own_partial[micro] + part.astype(F32)).astype(BF16))
        ctx_near.append(lax.ppermute(ctx[micro], BOTH, DEC_TO_ENC))
        ctx_own.append(lax.ppermute(ctx_near[micro], BOTH, ENC_SWAP))

    def attended(flags, sent, held, operands):
        grads = []
        for micro in micros:
            came = sent[micro]
            if micro > 0:
                came, grads[-1] = lax.optimization_barrier((came, grads[-1]))
            grads.append(attend(flags, (came, *held[micro : micro + 1]), *operands, micro))
        return zip(*grads)

    dq, dk, dv = attended(near_flags, ctx_near, ctx, near)
    far_dq = []
    for micro in micros:
        far_dq.append(lax.ppermute(dq[micro], BOTH, DEC_SWAP))
    own_dk, own_dv = attended(own_flags, ctx_own, (), own)

    def chip_sums(grads):
        give = projected(give_at, dec[None], grads, first, second)
        other = lax.ppermute(give, "segment", CORE_SWAP)
        return projected(keep_at, dec[None], grads, first, second, other)

    def reduced(blocks, result):
        for step, block in zip(STEPS, blocks):
            pairs = [(2 * x + k, 2 * ((x + step) % 4) + k) for x in range(4) for k in range(2)]
            other = lax.ppermute(block, "segment", pairs)
            result = result + other.astype(F32)
        return result.astype(BF16)

    *blocks, block = chip_sums((*far_dq, *dk, *dv))
    own_grads = (*dq, *own_dk, *own_dv)
    from_partner = lax.ppermute(reduced(blocks, block), "fsdp", HALF_SWAP)
    *blocks, block = chip_sums(own_grads)
    own_out = reduced(blocks, block)
    result = jnp.where(
        half == 0,
        jnp.concatenate([own_out, from_partner], axis=1),
        jnp.concatenate([from_partner, own_out], axis=1),
    )
    return result.reshape(1, micro_count, reaction_count, seq_length, 2 * shard_rows)


def solution(mesh):
    return jax.shard_map(
        per_device,
        mesh=mesh,
        in_specs=(
            P(None, "fsdp", None, None),
            P(None, "fsdp", None, "segment"),
            P(None, "fsdp", None, "segment"),
            P(None, "fsdp", None, "segment"),
            P(None, "fsdp", None),
            P("section", None, "fsdp", "segment"),
        ),
        out_specs=P("section", None, "fsdp", None, "segment"),
        check_vma=False,
    )
```

```python
import functools

import jax
import jax.numpy as jnp
from jax import lax
from jax.experimental import pallas as pl
from jax.experimental.pallas import tpu as pltpu
from jax.sharding import PartitionSpec as P


HDIM = 128

Z_LINES = [[2 * z + half for z in range(8)] for half in range(2)]
DEC_SWAP = [(16 + f, 16 + (f ^ 1)) for f in range(16)]
ENC_SWAP = [(f, f ^ 1) for f in range(16)]
DEC_TO_ENC = [(16 + f, f ^ 1) for f in range(16)]
HALF_SWAP = [(f, f ^ 1) for f in range(16)]
CORE_SWAP = [(g, g ^ 1) for g in range(8)]
BOTH = ("section", "fsdp")
STEPS = (2, 1, 3, 0)
F32 = jnp.float32
HBM = pl.BlockSpec(memory_space=pltpu.HBM)
BF16 = jnp.bfloat16
NT = (((1,), (1,)), ((), ()))
TN = (((0,), (0,)), ((), ()))
NN = (((1,), (0,)), ((), ()))


def mm(left, right, dims):
    return lax.dot_general(left, right, dims, preferred_element_type=F32)


def cost(flops, bytes_accessed):
    return pl.CostEstimate(flops=flops, bytes_accessed=bytes_accessed, transcendentals=0)


def pick_kernel(where, source, target):
    target[...] = source[...]


def picked(source, columns, width):
    rows = source.shape[0]
    count = columns.shape[0]
    return pl.pallas_call(
        pick_kernel,
        grid_spec=pltpu.PrefetchScalarGridSpec(
            num_scalar_prefetch=1,
            grid=(count,),
            in_specs=[pl.BlockSpec((rows, width), lambda i, at: (0, at[i]))],
            out_specs=pl.BlockSpec((rows, width), lambda i, at: (0, i)),
        ),
        out_shape=jax.ShapeDtypeStruct((rows, count * width), source.dtype),
        cost_estimate=cost(0, 2 * rows * count * width * 2),
        name="pick",
    )(columns, source)


def fetched(step, weight, buffer, sems):
    rows = weight.shape[1]
    copies = [
        pltpu.make_async_copy(weight.at[z], buffer.at[pl.ds(z * rows, rows)], sems.at[z])
        for z in range(8)
    ]

    @pl.when(step == 0)
    def _():
        for copy in copies:
            copy.start()

    for j in range(4):

        @pl.when(step == j)
        def _():
            copies[2 * j].wait()
            copies[2 * j + 1].wait()

    return buffer[pl.ds(pl.multiple_of(step * 2 * rows, 2 * rows), 2 * rows), :]


def added(step, acc, part):
    @pl.when(step == 0)
    def _():
        acc[...] = part

    @pl.when(step > 0)
    def _():
        acc[...] += part


def far_kernel(core, came, twin, weight, low, high, acc, buffer, sems):
    step = pl.program_id(0)
    rows = jnp.where(core[0] == step // 2, came[...], twin[...])
    added(step, acc, mm(rows, fetched(step, weight, buffer, sems), NN))

    @pl.when(step == pl.num_programs(0) - 1)
    def _():
        rows = low.shape[0]
        low[...] = acc[:rows].astype(BF16)
        high[...] = acc[rows:].astype(BF16)


def near_kernel(half, first, second, weight, low, high, buffer, sems):
    step = pl.program_id(0)
    rows = jnp.concatenate([first[...], second[...]], axis=1)
    part = mm(rows, fetched(step, weight, buffer, sems), NN)
    count = low.shape[0]
    added(step, low, part[:count])
    added(step, high, part[count:])


def partial_products(scalars, operands, specs, weight, out_dtype, kernel):
    row_count = operands[0].shape[0]
    _, shard, width = weight.shape
    extra = [pltpu.VMEM((row_count, width), F32)] if out_dtype == BF16 else []
    return pl.pallas_call(
        kernel,
        grid_spec=pltpu.PrefetchScalarGridSpec(
            num_scalar_prefetch=1,
            grid=(4,),
            in_specs=specs + [HBM],
            out_specs=[pl.BlockSpec((row_count // 2, width), lambda j, at: (0, 0))] * 2,
            scratch_shapes=extra
            + [pltpu.VMEM((8 * shard, width), BF16), pltpu.SemaphoreType.DMA((8,))],
        ),
        out_shape=[jax.ShapeDtypeStruct((row_count // 2, width), out_dtype)] * 2,
        cost_estimate=cost(2 * row_count * 8 * shard * width, 2 * 8 * shard * width),
    )(scalars, *operands, weight)


def attend_kernel(heads, flags, *refs):
    *sent, query, key, value, mask, dq, dk, dv = refs if len(refs) > 8 else (*refs[:5], None, *refs[5:])
    scale = HDIM ** (-0.5)
    cuts = [slice(head * HDIM, (head + 1) * HDIM) for head in range(heads)]

    def grads_of(cut):
        grad = sent[0][:, cut]
        if len(sent) > 1:
            grad = jnp.where(flags[0] > 0, sent[1][:, cut], grad)
        q, k, v = query[:, cut], key[:, cut], value[:, cut]
        scores = jnp.where(mask[:, :1] > 0, mm(k, q, NT) * scale, -jnp.inf)
        raised = jnp.exp(scores - jnp.max(scores, axis=0, keepdims=True))
        probs = raised * (1.0 / jnp.sum(raised, axis=0, keepdims=True))
        prob_grad = mm(v, grad, NT)
        center = jnp.sum(probs * prob_grad, axis=0, keepdims=True)
        return grad, q, k, probs, (probs * (prob_grad - center)).astype(BF16)

    def query_grads():
        for cut in cuts:
            _, _, k, _, score_grad = grads_of(cut)
            dq[:, cut] = (mm(score_grad, k, TN) * scale).astype(BF16)

    def key_value_grads():
        for cut in cuts:
            grad, q, _, probs, score_grad = grads_of(cut)
            dk[:, cut] = (mm(score_grad, q, NN) * scale).astype(BF16)
            dv[:, cut] = mm(probs.astype(BF16), grad, NN).astype(BF16)

    if len(sent) > 1:
        pl.when(flags[0] > 0)(query_grads)
    pl.when(flags[1] > 0)(key_value_grads)


def attend(flags, sent, query, key, value, mask, micro):
    seq_length, width = sent[0].shape
    heads = 2
    wide = heads * HDIM
    one = pl.BlockSpec((seq_length, wide), lambda h, flags: (0, h))
    row = pl.BlockSpec((None, seq_length, wide), lambda h, flags: (micro, 0, h))
    out = jax.ShapeDtypeStruct((seq_length, width), BF16)
    outs = 1 + len(sent)
    return pl.pallas_call(
        functools.partial(attend_kernel, heads),
        grid_spec=pltpu.PrefetchScalarGridSpec(
            num_scalar_prefetch=1,
            grid=(width // wide,),
            in_specs=[one] * len(sent)
            + [
                row,
                row,
                row,
                pl.BlockSpec((None, seq_length, HDIM), lambda h, flags: (micro, 0, 0)),
            ],
            out_specs=[one] * outs,
        ),
        out_shape=[out] * outs,
        cost_estimate=cost(
            10 * seq_length * seq_length * width, 16 * seq_length * width
        ),
        name="attend",
    )(flags, *sent, query, key, value, mask)


def products(count, at, flags, refs):
    weights = refs[3 * count : 3 * count + 2]
    total, buffer, sems = refs[-3:]
    step = pl.program_id(0)
    encoder = flags[0] == 0

    def rows(kind):
        return jnp.concatenate([x[...] for x in refs[kind * count : (kind + 1) * count]])

    def copy(which, place):
        return pltpu.make_async_copy(
            weights[which].at[at[place]], buffer.at[which, place], sems.at[which, place]
        )

    def wide(which):
        pair = buffer[which, pl.ds(2 * step, 2)]
        return pair.reshape(pair.shape[0] * pair.shape[1], pair.shape[2])

    @pl.when(step == 0)
    def _():
        for place in range(4):
            copy(1, place).start()

            @pl.when(encoder)
            def _():
                copy(0, place).start()

    copy(1, 2 * step).wait()
    copy(1, 2 * step + 1).wait()
    total[...] = mm(jnp.where(encoder, rows(2), rows(0)), wide(1), NT)

    @pl.when(encoder)
    def _():
        copy(0, 2 * step).wait()
        copy(0, 2 * step + 1).wait()
        total[...] += mm(rows(1), wide(0), NT)

    return total


def give_kernel(count, at, flags, *refs):
    out = refs[3 * count + 2]
    total = products(count, at, flags, refs)
    shard = out.shape[2]
    for place in range(2):
        out[place] = total[:, place * shard : (place + 1) * shard].astype(BF16)


def keep_kernel(count, at, flags, *refs):
    other, outs = refs[3 * count + 2], refs[3 * count + 3 : 3 * count + 7]
    total = products(count, at, flags, refs)
    shard = outs[0].shape[1]
    for i, out in enumerate(outs):

        @pl.when(pl.program_id(0) == i // 2)
        def _():
            cut = slice(i % 2 * shard, (i % 2 + 1) * shard)
            out[...] = (total[:, cut] + other[i % 2].astype(F32)).astype(out.dtype)


def projected(at, flags, grads, first, second, other=None):
    count = len(grads) // 3
    rows, width = grads[0].shape
    shard = first.shape[1]
    operand = pl.BlockSpec((rows, width), lambda i, at, flags: (0, 0))
    moving = pl.BlockSpec((2, count * rows, shard), lambda i, at, flags: (i, 0, 0))
    fixed = pl.BlockSpec((count * rows, shard), lambda i, at, flags: (0, 0))
    if other is None:
        kernel, extra = give_kernel, ()
        out_specs = moving
        out_shape = jax.ShapeDtypeStruct((4, count * rows, shard), BF16)
    else:
        kernel, extra = keep_kernel, (other,)
        out_specs = [fixed] * 4
        out_shape = [
            jax.ShapeDtypeStruct((count * rows, shard), t) for t in (BF16, BF16, BF16, F32)
        ]
    return pl.pallas_call(
        functools.partial(kernel, count),
        grid_spec=pltpu.PrefetchScalarGridSpec(
            num_scalar_prefetch=2,
            grid=(2,),
            in_specs=[operand] * len(grads) + [HBM] * 2 + [moving] * len(extra),
            out_specs=out_specs,
            scratch_shapes=[
                pltpu.VMEM((count * rows, 2 * shard), F32),
                pltpu.VMEM((2, 4, shard, width), BF16),
                pltpu.SemaphoreType.DMA((2, 4)),
            ],
        ),
        out_shape=out_shape,
        cost_estimate=cost(
            2 * count * rows * 2 * width * 4 * shard, 2 * 2 * 4 * shard * width
        ),
    )(at, flags, *grads, first, second, *extra)


def per_device(out_grad, queries, enc_keys, enc_values, key_mask, weights):
    decoder = lax.axis_index("section") == 1
    half = lax.axis_index("fsdp") % 2
    segment = lax.axis_index("segment")
    core = segment % 2
    chip = segment // 2
    micro_count, reaction_count, seq_length, feature_width = out_grad.shape
    local_width = queries.shape[3]
    shard_rows = weights.shape[2]
    row_count = micro_count * reaction_count * seq_length
    flat = (micro_count, seq_length, local_width)
    micros = range(micro_count)
    dec = decoder.astype(jnp.int32)

    def gathered(shard):
        return lax.all_gather(shard, "fsdp", axis=0, axis_index_groups=Z_LINES)

    own = (
        queries.reshape(flat),
        enc_keys.reshape(flat),
        enc_values.reshape(flat),
        key_mask.reshape(micro_count, 1, seq_length),
    )
    came_near = []
    for value in own:
        came_near.append(lax.ppermute(value, BOTH, ENC_SWAP))
    near = [jnp.where(decoder, mine, other) for mine, other in zip(own, came_near)]
    near[3], own_mask = [
        jnp.broadcast_to(mask.reshape(micro_count, seq_length, 1), (micro_count, seq_length, HDIM))
        for mask in (near[3], own[3])
    ]

    near_flags = jnp.stack([dec, 1 - dec])
    own_flags = jnp.stack([0 * dec, 1 - dec])
    places = 2 * ((chip + jnp.array(STEPS, jnp.int32)) % 4)
    keep_at, give_at = places + core, places + 1 - core

    grads = out_grad.reshape(row_count, feature_width)
    columns = 2 * (4 * core + jnp.arange(4, dtype=jnp.int32)) + 1 - half
    first = gathered(weights[0, 0])
    part = picked(grads, columns, shard_rows)
    part, later_weights = lax.optimization_barrier((part, weights))
    second = gathered(later_weights[0, 1])
    came = lax.ppermute(part, BOTH, DEC_SWAP)
    twin = lax.ppermute(came, "segment", CORE_SWAP)

    ready = (came, twin, near, own_mask, near_flags, own_flags, keep_at, give_at)
    first, ready = lax.optimization_barrier((first, ready))
    came, twin, near, own_mask, near_flags, own_flags, keep_at, give_at = ready
    own = (*own[:3], own_mask)

    piece = 2 * shard_rows
    moved = pl.BlockSpec((row_count, piece), lambda j, at: (0, j % 2))
    far = []
    for partial in partial_products(core[None], (came, twin), [moved] * 2, first, BF16, far_kernel):
        far.append(lax.ppermute(partial, BOTH, DEC_SWAP))
    own_partial = partial_products(
        half[None],
        (grads, grads),
        [
            pl.BlockSpec((row_count, shard_rows), lambda j, half: (0, 4 * j + half[0])),
            pl.BlockSpec((row_count, shard_rows), lambda j, half: (0, 4 * j + 2 + half[0])),
        ],
        first,
        F32,
        near_kernel,
    )
    ctx, ctx_near, ctx_own = [], [], []
    for micro in micros:
        part = far[micro]
        if micro > 0:
            part, ctx[-1] = lax.optimization_barrier((part, ctx[-1]))
        ctx.append((own_partial[micro] + part.astype(F32)).astype(BF16))
        ctx_near.append(lax.ppermute(ctx[micro], BOTH, DEC_TO_ENC))
        ctx_own.append(lax.ppermute(ctx_near[micro], BOTH, ENC_SWAP))

    def attended(flags, sent, held, operands):
        grads = []
        for micro in micros:
            came = sent[micro]
            if micro > 0:
                came, grads[-1] = lax.optimization_barrier((came, grads[-1]))
            grads.append(attend(flags, (came, *held[micro : micro + 1]), *operands, micro))
        return zip(*grads)

    dq, dk, dv = attended(near_flags, ctx_near, ctx, near)
    far_dq = []
    for micro in micros:
        far_dq.append(lax.ppermute(dq[micro], BOTH, DEC_SWAP))
    own_dk, own_dv = attended(own_flags, ctx_own, (), own)

    def chip_sums(grads):
        give = projected(give_at, dec[None], grads, first, second)
        other = lax.ppermute(give, "segment", CORE_SWAP)
        return projected(keep_at, dec[None], grads, first, second, other)

    def reduced(blocks, result):
        for step, block in zip(STEPS, blocks):
            pairs = [(2 * x + k, 2 * ((x + step) % 4) + k) for x in range(4) for k in range(2)]
            other = lax.ppermute(block, "segment", pairs)
            result = result + other.astype(F32)
        return result.astype(BF16)

    *blocks, block = chip_sums((*far_dq, dq[0], *dk, own_dk[0], *dv, own_dv[0]))
    early = reduced(blocks, block)
    from_partner = lax.ppermute(early[:row_count], "fsdp", HALF_SWAP)
    *blocks, block = chip_sums((dq[1], own_dk[1], own_dv[1]))
    own_out = jnp.concatenate([early[row_count:], reduced(blocks, block)])
    result = jnp.where(
        half == 0,
        jnp.concatenate([own_out, from_partner], axis=1),
        jnp.concatenate([from_partner, own_out], axis=1),
    )
    return result.reshape(1, micro_count, reaction_count, seq_length, 2 * shard_rows)


def solution(mesh):
    return jax.shard_map(
        per_device,
        mesh=mesh,
        in_specs=(
            P(None, "fsdp", None, None),
            P(None, "fsdp", None, "segment"),
            P(None, "fsdp", None, "segment"),
            P(None, "fsdp", None, "segment"),
            P(None, "fsdp", None),
            P("section", None, "fsdp", "segment"),
        ),
        out_specs=P("section", None, "fsdp", None, "segment"),
        check_vma=False,
    )
```

```python
import functools

import jax
import jax.numpy as jnp
from jax import lax
from jax.experimental import pallas as pl
from jax.experimental.pallas import tpu as pltpu
from jax.sharding import PartitionSpec as P


HDIM = 128

Z_LINES = [[2 * z + half for z in range(8)] for half in range(2)]
DEC_SWAP = [(16 + f, 16 + (f ^ 1)) for f in range(16)]
ENC_SWAP = [(f, f ^ 1) for f in range(16)]
DEC_TO_ENC = [(16 + f, f ^ 1) for f in range(16)]
HALF_SWAP = [(f, f ^ 1) for f in range(16)]
CORE_SWAP = [(g, g ^ 1) for g in range(8)]
BOTH = ("section", "fsdp")
STEPS = (2, 1, 3, 0)
F32 = jnp.float32
HBM = pl.BlockSpec(memory_space=pltpu.HBM)
BF16 = jnp.bfloat16
NT = (((1,), (1,)), ((), ()))
TN = (((0,), (0,)), ((), ()))
NN = (((1,), (0,)), ((), ()))


def mm(left, right, dims):
    return lax.dot_general(left, right, dims, preferred_element_type=F32)


def cost(flops, bytes_accessed):
    return pl.CostEstimate(flops=flops, bytes_accessed=bytes_accessed, transcendentals=0)


def pick_kernel(where, source, target):
    target[...] = source[...]


def picked(source, columns, width):
    rows = source.shape[0]
    count = columns.shape[0]
    return pl.pallas_call(
        pick_kernel,
        grid_spec=pltpu.PrefetchScalarGridSpec(
            num_scalar_prefetch=1,
            grid=(count,),
            in_specs=[pl.BlockSpec((rows, width), lambda i, at: (0, at[i]))],
            out_specs=pl.BlockSpec((rows, width), lambda i, at: (0, i)),
        ),
        out_shape=jax.ShapeDtypeStruct((rows, count * width), source.dtype),
        cost_estimate=cost(0, 2 * rows * count * width * 2),
        name="pick",
    )(columns, source)


def fetched(step, weight, buffer, sems):
    rows = weight.shape[1]
    copies = [
        pltpu.make_async_copy(weight.at[z], buffer.at[pl.ds(z * rows, rows)], sems.at[z])
        for z in range(8)
    ]

    @pl.when(step == 0)
    def _():
        for copy in copies:
            copy.start()

    for j in range(4):

        @pl.when(step == j)
        def _():
            copies[2 * j].wait()
            copies[2 * j + 1].wait()

    return buffer[pl.ds(pl.multiple_of(step * 2 * rows, 2 * rows), 2 * rows), :]


def added(step, acc, part):
    @pl.when(step == 0)
    def _():
        acc[...] = part

    @pl.when(step > 0)
    def _():
        acc[...] += part


def far_kernel(core, came, twin, weight, low, high, acc, buffer, sems):
    step = pl.program_id(0)
    rows = jnp.where(core[0] == step // 2, came[...], twin[...])
    added(step, acc, mm(rows, fetched(step, weight, buffer, sems), NN))

    @pl.when(step == pl.num_programs(0) - 1)
    def _():
        rows = low.shape[0]
        low[...] = acc[:rows].astype(BF16)
        high[...] = acc[rows:].astype(BF16)


def near_kernel(half, first, second, weight, low, high, buffer, sems):
    step = pl.program_id(0)
    rows = jnp.concatenate([first[...], second[...]], axis=1)
    part = mm(rows, fetched(step, weight, buffer, sems), NN)
    count = low.shape[0]
    added(step, low, part[:count])
    added(step, high, part[count:])


def partial_products(scalars, operands, specs, weight, out_dtype, kernel):
    row_count = operands[0].shape[0]
    _, shard, width = weight.shape
    extra = [pltpu.VMEM((row_count, width), F32)] if out_dtype == BF16 else []
    return pl.pallas_call(
        kernel,
        grid_spec=pltpu.PrefetchScalarGridSpec(
            num_scalar_prefetch=1,
            grid=(4,),
            in_specs=specs + [HBM],
            out_specs=[pl.BlockSpec((row_count // 2, width), lambda j, at: (0, 0))] * 2,
            scratch_shapes=extra
            + [pltpu.VMEM((8 * shard, width), BF16), pltpu.SemaphoreType.DMA((8,))],
        ),
        out_shape=[jax.ShapeDtypeStruct((row_count // 2, width), out_dtype)] * 2,
        cost_estimate=cost(2 * row_count * 8 * shard * width, 2 * 8 * shard * width),
    )(scalars, *operands, weight)


def attend_kernel(heads, flags, *refs):
    *sent, query, key, value, hidden, first_out, second_out = refs
    scale = HDIM ** (-0.5)
    cuts = [slice(head * HDIM, (head + 1) * HDIM) for head in range(heads)]

    def grads_of(cut):
        grad = sent[0][:, cut]
        if len(sent) > 1:
            grad = jnp.where(flags[0] > 0, sent[1][:, cut], grad)
        q, k, v = query[:, cut], key[:, cut], value[:, cut]
        scores = mm(k, q, NT) * scale + jnp.concatenate([hidden[...]] * 2, axis=1)
        prob_grad = mm(v, grad, NT)
        raised = jnp.exp(scores - jnp.max(scores, axis=0, keepdims=True))
        share = 1.0 / jnp.sum(raised, axis=0, keepdims=True)
        center = jnp.sum(raised * prob_grad, axis=0, keepdims=True) * share
        probs = raised * share
        return grad, q, k, probs, (probs * (prob_grad - center)).astype(BF16)

    def query_grads():
        for cut in cuts:
            _, _, k, _, score_grad = grads_of(cut)
            second_out[:, cut] = (mm(score_grad, k, TN) * scale).astype(BF16)

    def key_value_grads():
        for cut in cuts:
            grad, q, _, probs, score_grad = grads_of(cut)
            first_out[:, cut] = (mm(score_grad, q, NN) * scale).astype(BF16)
            second_out[:, cut] = mm(probs.astype(BF16), grad, NN).astype(BF16)

    if len(sent) > 1:
        pl.when(flags[0] > 0)(query_grads)
    pl.when(flags[1] > 0)(key_value_grads)


def attend(flags, sent, query, key, value, mask, micro):
    seq_length, width = sent[0].shape
    heads = 2
    wide = heads * HDIM
    one = pl.BlockSpec((seq_length, wide), lambda h, flags: (0, h))
    row = pl.BlockSpec((None, seq_length, wide), lambda h, flags: (micro, 0, h))
    out = jax.ShapeDtypeStruct((seq_length, width), BF16)
    return pl.pallas_call(
        functools.partial(attend_kernel, heads),
        grid_spec=pltpu.PrefetchScalarGridSpec(
            num_scalar_prefetch=1,
            grid=(width // wide,),
            in_specs=[one] * len(sent)
            + [
                row,
                row,
                row,
                pl.BlockSpec((None, seq_length, HDIM), lambda h, flags: (micro, 0, 0)),
            ],
            out_specs=[one] * 2,
        ),
        out_shape=[out] * 2,
        cost_estimate=cost(
            10 * seq_length * seq_length * width, 16 * seq_length * width
        ),
        name="attend",
    )(flags, *sent, query, key, value, mask)


def products(count, at, flags, refs):
    kinds = [refs[kind * count : (kind + 1) * count] for kind in range(3)]
    weights = refs[3 * count : 3 * count + 2]
    total, rows, row_sems, buffer, sems = refs[-5:]
    each = rows.shape[1] // count
    step = pl.program_id(0)
    encoder = flags[0] == 0

    def row_copy(kind, which, i):
        return pltpu.make_async_copy(
            kinds[kind][i], rows.at[which, pl.ds(i * each, each)], row_sems.at[which, i]
        )

    def copy(which, place):
        return pltpu.make_async_copy(
            weights[which].at[at[place]], buffer.at[which, place], sems.at[which, place]
        )

    def wide(which):
        pair = buffer[which, pl.ds(2 * step, 2)]
        return pair.reshape(pair.shape[0] * pair.shape[1], pair.shape[2])

    @pl.when((step == 0) & encoder)
    def _():
        for turn in range(2):
            for which, kind in ((1, 2), (0, 1)):
                for i in range(count if turn == 0 else 0):
                    row_copy(kind, which, i).start()
                copy(which, 2 * turn).start()
                copy(which, 2 * turn + 1).start()
        for i in range(count):
            row_copy(2, 1, i).wait()

    @pl.when((step == 0) & (flags[0] > 0))
    def _():
        for i in range(count):
            row_copy(0, 1, i).start()
        for place in range(4):
            copy(1, place).start()
        for i in range(count):
            row_copy(0, 1, i).wait()

    copy(1, 2 * step).wait()
    copy(1, 2 * step + 1).wait()
    total[...] = mm(rows[1], wide(1), NT)

    @pl.when((step == 0) & encoder)
    def _():
        for i in range(count):
            row_copy(1, 0, i).wait()

    @pl.when(encoder)
    def _():
        copy(0, 2 * step).wait()
        copy(0, 2 * step + 1).wait()
        total[...] += mm(rows[0], wide(0), NT)

    return total


def give_kernel(count, at, flags, *refs):
    out = refs[3 * count + 2]
    total = products(count, at, flags, refs)
    shard = out.shape[2]
    for place in range(2):
        out[place] = total[:, place * shard : (place + 1) * shard].astype(BF16)


def keep_kernel(count, at, flags, *refs):
    other, outs = refs[3 * count + 2], refs[3 * count + 3 : 3 * count + 7]
    total = products(count, at, flags, refs)
    shard = outs[0].shape[1]
    for i, out in enumerate(outs):

        @pl.when(pl.program_id(0) == i // 2)
        def _():
            cut = slice(i % 2 * shard, (i % 2 + 1) * shard)
            out[...] = (total[:, cut] + other[i % 2].astype(F32)).astype(out.dtype)


def projected(at, flags, grads, first, second, other=None):
    count = len(grads) // 3
    rows, width = grads[0].shape
    shard = first.shape[1]
    moving = pl.BlockSpec((2, count * rows, shard), lambda i, at, flags: (i, 0, 0))
    fixed = pl.BlockSpec((count * rows, shard), lambda i, at, flags: (0, 0))
    if other is None:
        kernel, extra = give_kernel, ()
        out_specs = moving
        out_shape = jax.ShapeDtypeStruct((4, count * rows, shard), BF16)
    else:
        kernel, extra = keep_kernel, (other,)
        out_specs = [fixed] * 4
        out_shape = [
            jax.ShapeDtypeStruct((count * rows, shard), t) for t in (BF16, BF16, BF16, F32)
        ]
    return pl.pallas_call(
        functools.partial(kernel, count),
        grid_spec=pltpu.PrefetchScalarGridSpec(
            num_scalar_prefetch=2,
            grid=(2,),
            in_specs=[HBM] * (len(grads) + 2) + [moving] * len(extra),
            out_specs=out_specs,
            scratch_shapes=[
                pltpu.VMEM((count * rows, 2 * shard), F32),
                pltpu.VMEM((2, count * rows, width), BF16),
                pltpu.SemaphoreType.DMA((2, count)),
                pltpu.VMEM((2, 4, shard, width), BF16),
                pltpu.SemaphoreType.DMA((2, 4)),
            ],
        ),
        out_shape=out_shape,
        cost_estimate=cost(
            2 * count * rows * 2 * width * 4 * shard, 2 * 2 * 4 * shard * width
        ),
    )(at, flags, *grads, first, second, *extra)


def per_device(out_grad, queries, enc_keys, enc_values, key_mask, weights):
    decoder = lax.axis_index("section") == 1
    half = lax.axis_index("fsdp") % 2
    segment = lax.axis_index("segment")
    core = segment % 2
    chip = segment // 2
    micro_count, reaction_count, seq_length, feature_width = out_grad.shape
    local_width = queries.shape[3]
    shard_rows = weights.shape[2]
    row_count = micro_count * reaction_count * seq_length
    flat = (micro_count, seq_length, local_width)
    micros = range(micro_count)
    dec = decoder.astype(jnp.int32)

    def gathered(shard):
        return lax.all_gather(shard, "fsdp", axis=0, axis_index_groups=Z_LINES)

    own = (
        queries.reshape(flat),
        enc_keys.reshape(flat),
        enc_values.reshape(flat),
        jnp.broadcast_to(
            jnp.where(key_mask > 0, 0.0, -jnp.inf).astype(F32).reshape(micro_count, seq_length, 1),
            (micro_count, seq_length, HDIM),
        ),
    )
    came_near = []
    for value in own:
        came_near.append(lax.ppermute(value, BOTH, ENC_SWAP))
    near = [jnp.where(decoder, mine, other) for mine, other in zip(own, came_near)]
    near_flags = jnp.stack([dec, 1 - dec])
    own_flags = jnp.stack([0 * dec, 1 - dec])
    places = 2 * ((chip + jnp.array(STEPS, jnp.int32)) % 4)
    keep_at, give_at = places + core, places + 1 - core

    grads = out_grad.reshape(row_count, feature_width)
    columns = 2 * (4 * core + jnp.arange(4, dtype=jnp.int32)) + 1 - half
    first = gathered(weights[0, 0])
    part = picked(grads, columns, shard_rows)
    part, later_weights = lax.optimization_barrier((part, weights))
    second = gathered(later_weights[0, 1])
    came = lax.ppermute(part, BOTH, DEC_SWAP)
    twin = lax.ppermute(came, "segment", CORE_SWAP)

    ready = (came, twin, near, own[3], near_flags, own_flags, keep_at, give_at)
    first, ready = lax.optimization_barrier((first, ready))
    came, twin, near, own_mask, near_flags, own_flags, keep_at, give_at = ready
    own = (*own[:3], own_mask)

    piece = 2 * shard_rows
    moved = pl.BlockSpec((row_count, piece), lambda j, at: (0, j % 2))
    far = []
    for partial in partial_products(core[None], (came, twin), [moved] * 2, first, BF16, far_kernel):
        far.append(lax.ppermute(partial, BOTH, DEC_SWAP))
    own_partial = partial_products(
        half[None],
        (grads, grads),
        [
            pl.BlockSpec((row_count, shard_rows), lambda j, half: (0, 4 * j + half[0])),
            pl.BlockSpec((row_count, shard_rows), lambda j, half: (0, 4 * j + 2 + half[0])),
        ],
        first,
        F32,
        near_kernel,
    )
    ctx, ctx_near, ctx_own = [], [], []
    for micro in micros:
        part = far[micro]
        if micro > 0:
            part, ctx[-1] = lax.optimization_barrier((part, ctx[-1]))
        ctx.append((own_partial[micro] + part.astype(F32)).astype(BF16))
        ctx_near.append(lax.ppermute(ctx[micro], BOTH, DEC_TO_ENC))
        ctx_own.append(lax.ppermute(ctx_near[micro], BOTH, ENC_SWAP))

    def attended(flags, sent, held, operands):
        grads = []
        for micro in micros:
            came = sent[micro]
            if micro > 0:
                came, grads[-1] = lax.optimization_barrier((came, grads[-1]))
            grads.append(attend(flags, (came, *held[micro : micro + 1]), *operands, micro))
        return zip(*grads)

    dk, dv = attended(near_flags, ctx_near, ctx, near)
    far_dq = []
    for micro in micros:
        far_dq.append(lax.ppermute(dv[micro], BOTH, DEC_SWAP))
    own_dk, own_dv = attended(own_flags, ctx_own, (), own)

    def chip_sums(grads):
        give = projected(give_at, dec[None], grads, first, second)
        other = lax.ppermute(give, "segment", CORE_SWAP)
        return projected(keep_at, dec[None], grads, first, second, other)

    def reduced(blocks, result):
        for step, block in zip(STEPS, blocks):
            pairs = [(2 * x + k, 2 * ((x + step) % 4) + k) for x in range(4) for k in range(2)]
            other = lax.ppermute(block, "segment", pairs)
            result = result + other.astype(F32)
        return result.astype(BF16)

    *blocks, block = chip_sums((*far_dq, dv[0], *dk, own_dk[0], *dv, own_dv[0]))
    early = reduced(blocks, block)
    from_partner = lax.ppermute(early[:row_count], "fsdp", HALF_SWAP)
    *blocks, block = chip_sums((dv[1], own_dk[1], own_dv[1]))
    own_out = jnp.concatenate([early[row_count:], reduced(blocks, block)])
    result = jnp.where(
        half == 0,
        jnp.concatenate([own_out, from_partner], axis=1),
        jnp.concatenate([from_partner, own_out], axis=1),
    )
    return result.reshape(1, micro_count, reaction_count, seq_length, 2 * shard_rows)


def solution(mesh):
    return jax.shard_map(
        per_device,
        mesh=mesh,
        in_specs=(
            P(None, "fsdp", None, None),
            P(None, "fsdp", None, "segment"),
            P(None, "fsdp", None, "segment"),
            P(None, "fsdp", None, "segment"),
            P(None, "fsdp", None),
            P("section", None, "fsdp", "segment"),
        ),
        out_specs=P("section", None, "fsdp", None, "segment"),
        check_vma=False,
    )
```

```python
import functools

import jax
import jax.numpy as jnp
from jax import lax
from jax.experimental import pallas as pl
from jax.experimental.pallas import tpu as pltpu
from jax.sharding import PartitionSpec as P


HDIM = 128

Z_LINES = [[2 * z + half for z in range(8)] for half in range(2)]
DEC_SWAP = [(16 + f, 16 + (f ^ 1)) for f in range(16)]
ENC_SWAP = [(f, f ^ 1) for f in range(16)]
DEC_TO_ENC = [(16 + f, f ^ 1) for f in range(16)]
HALF_SWAP = [(f, f ^ 1) for f in range(16)]
CORE_SWAP = [(g, g ^ 1) for g in range(8)]
BOTH = ("section", "fsdp")
STEPS = (2, 1, 3, 0)
F32 = jnp.float32
HBM = pl.BlockSpec(memory_space=pltpu.HBM)
BF16 = jnp.bfloat16
NT = (((1,), (1,)), ((), ()))
TN = (((0,), (0,)), ((), ()))
NN = (((1,), (0,)), ((), ()))


def mm(left, right, dims):
    return lax.dot_general(left, right, dims, preferred_element_type=F32)


def cost(flops, bytes_accessed):
    return pl.CostEstimate(flops=flops, bytes_accessed=bytes_accessed, transcendentals=0)


def pick_kernel(where, source, target):
    target[...] = source[...]


def picked(source, columns, width):
    rows = source.shape[0]
    count = columns.shape[0]
    return pl.pallas_call(
        pick_kernel,
        grid_spec=pltpu.PrefetchScalarGridSpec(
            num_scalar_prefetch=1,
            grid=(count,),
            in_specs=[pl.BlockSpec((rows, width), lambda i, at: (0, at[i]))],
            out_specs=pl.BlockSpec((rows, width), lambda i, at: (0, i)),
        ),
        out_shape=jax.ShapeDtypeStruct((rows, count * width), source.dtype),
        cost_estimate=cost(0, 2 * rows * count * width * 2),
        name="pick",
    )(columns, source)


def fetched(step, weight, buffer, sems):
    rows = weight.shape[1]
    copies = [
        pltpu.make_async_copy(weight.at[z], buffer.at[pl.ds(z * rows, rows)], sems.at[z])
        for z in range(8)
    ]

    @pl.when(step == 0)
    def _():
        for copy in copies:
            copy.start()

    for j in range(4):

        @pl.when(step == j)
        def _():
            copies[2 * j].wait()
            copies[2 * j + 1].wait()

    return buffer[pl.ds(pl.multiple_of(step * 2 * rows, 2 * rows), 2 * rows), :]


def added(step, acc, part):
    @pl.when(step == 0)
    def _():
        acc[...] = part

    @pl.when(step > 0)
    def _():
        acc[...] += part


def far_kernel(scalars, came, twin, weight, low, high, acc, buffer, sems):
    step = pl.program_id(0)

    @pl.when(scalars[1] > 0)
    def _():
        rows = jnp.where(scalars[0] == step // 2, came[...], twin[...])
        added(step, acc, mm(rows, fetched(step, weight, buffer, sems), NN))

        @pl.when(step == pl.num_programs(0) - 1)
        def _():
            count = low.shape[0]
            low[...] = acc[:count].astype(BF16)
            high[...] = acc[count:].astype(BF16)


def near_kernel(scalars, first, second, weight, low, high, buffer, sems):
    step = pl.program_id(0)

    @pl.when(scalars[1] > 0)
    def _():
        rows = jnp.concatenate([first[...], second[...]], axis=1)
        part = mm(rows, fetched(step, weight, buffer, sems), NN)
        count = low.shape[0]
        added(step, low, part[:count])
        added(step, high, part[count:])


def partial_products(scalars, operands, specs, weight, out_dtype, kernel):
    row_count = operands[0].shape[0]
    _, shard, width = weight.shape
    extra = [pltpu.VMEM((row_count, width), F32)] if out_dtype == BF16 else []
    return pl.pallas_call(
        kernel,
        grid_spec=pltpu.PrefetchScalarGridSpec(
            num_scalar_prefetch=1,
            grid=(4,),
            in_specs=specs + [HBM],
            out_specs=[pl.BlockSpec((row_count // 2, width), lambda j, at: (0, 0))] * 2,
            scratch_shapes=extra
            + [pltpu.VMEM((8 * shard, width), BF16), pltpu.SemaphoreType.DMA((8,))],
        ),
        out_shape=[jax.ShapeDtypeStruct((row_count // 2, width), out_dtype)] * 2,
        cost_estimate=cost(2 * row_count * 8 * shard * width, 2 * 8 * shard * width),
    )(scalars, *operands, weight)


def attend_kernel(heads, flags, *refs):
    *sent, query, key, value, hidden, first_out, second_out = refs
    scale = HDIM ** (-0.5)
    cuts = [slice(head * HDIM, (head + 1) * HDIM) for head in range(heads)]

    def grads_of(cut):
        grad = sent[0][:, cut]
        if len(sent) > 1:
            grad = jnp.where(flags[0] > 0, sent[1][:, cut], grad)
        q, k, v = query[:, cut], key[:, cut], value[:, cut]
        scores = mm(k, q, NT) * scale + jnp.concatenate([hidden[...]] * 2, axis=1)
        prob_grad = mm(v, grad, NT)
        raised = jnp.exp(scores - jnp.max(scores, axis=0, keepdims=True))
        share = 1.0 / jnp.sum(raised, axis=0, keepdims=True)
        center = jnp.sum(raised * prob_grad, axis=0, keepdims=True) * share
        probs = raised * share
        return grad, q, k, probs, (probs * (prob_grad - center)).astype(BF16)

    def query_grads():
        for cut in cuts:
            _, _, k, _, score_grad = grads_of(cut)
            second_out[:, cut] = (mm(score_grad, k, TN) * scale).astype(BF16)

    def key_value_grads():
        for cut in cuts:
            grad, q, _, probs, score_grad = grads_of(cut)
            first_out[:, cut] = (mm(score_grad, q, NN) * scale).astype(BF16)
            second_out[:, cut] = mm(probs.astype(BF16), grad, NN).astype(BF16)

    if len(sent) > 1:
        pl.when(flags[0] > 0)(query_grads)
    pl.when(flags[1] > 0)(key_value_grads)


def attend(flags, sent, query, key, value, mask, micro):
    seq_length, width = sent[0].shape
    heads = 2
    wide = heads * HDIM
    one = pl.BlockSpec((seq_length, wide), lambda h, flags: (0, h))
    row = pl.BlockSpec((None, seq_length, wide), lambda h, flags: (micro, 0, h))
    out = jax.ShapeDtypeStruct((seq_length, width), BF16)
    return pl.pallas_call(
        functools.partial(attend_kernel, heads),
        grid_spec=pltpu.PrefetchScalarGridSpec(
            num_scalar_prefetch=1,
            grid=(width // wide,),
            in_specs=[one] * len(sent)
            + [
                row,
                row,
                row,
                pl.BlockSpec((None, seq_length, HDIM), lambda h, flags: (micro, 0, 0)),
            ],
            out_specs=[one] * 2,
        ),
        out_shape=[out] * 2,
        cost_estimate=cost(
            10 * seq_length * seq_length * width, 16 * seq_length * width
        ),
        name="attend",
    )(flags, *sent, query, key, value, mask)


def products(count, at, flags, refs):
    kinds = [refs[kind * count : (kind + 1) * count] for kind in range(3)]
    weights = refs[3 * count : 3 * count + 2]
    total, rows, row_sems, buffer, sems = refs[-5:]
    each = rows.shape[1] // count
    step = pl.program_id(0)
    encoder = flags[0] == 0

    def row_copy(kind, which, i):
        return pltpu.make_async_copy(
            kinds[kind][i], rows.at[which, pl.ds(i * each, each)], row_sems.at[which, i]
        )

    def copy(which, place):
        return pltpu.make_async_copy(
            weights[which].at[at[place]], buffer.at[which, place], sems.at[which, place]
        )

    def wide(which):
        pair = buffer[which, pl.ds(2 * step, 2)]
        return pair.reshape(pair.shape[0] * pair.shape[1], pair.shape[2])

    @pl.when((step == 0) & encoder)
    def _():
        for turn in range(2):
            for which, kind in ((1, 2), (0, 1)):
                for i in range(count if turn == 0 else 0):
                    row_copy(kind, which, i).start()
                copy(which, 2 * turn).start()
                copy(which, 2 * turn + 1).start()
        for i in range(count):
            row_copy(2, 1, i).wait()

    @pl.when((step == 0) & (flags[0] > 0))
    def _():
        for i in range(count):
            row_copy(0, 1, i).start()
        for place in range(4):
            copy(1, place).start()
        for i in range(count):
            row_copy(0, 1, i).wait()

    copy(1, 2 * step).wait()
    copy(1, 2 * step + 1).wait()
    total[...] = mm(rows[1], wide(1), NT)

    @pl.when((step == 0) & encoder)
    def _():
        for i in range(count):
            row_copy(1, 0, i).wait()

    @pl.when(encoder)
    def _():
        copy(0, 2 * step).wait()
        copy(0, 2 * step + 1).wait()
        total[...] += mm(rows[0], wide(0), NT)

    return total


def give_kernel(count, at, flags, *refs):
    out = refs[3 * count + 2]
    total = products(count, at, flags, refs)
    shard = out.shape[2]
    for place in range(2):
        out[place] = total[:, place * shard : (place + 1) * shard].astype(BF16)


def keep_kernel(count, at, flags, *refs):
    other, outs = refs[3 * count + 2], refs[3 * count + 3 : 3 * count + 7]
    total = products(count, at, flags, refs)
    shard = outs[0].shape[1]
    for i, out in enumerate(outs):

        @pl.when(pl.program_id(0) == i // 2)
        def _():
            cut = slice(i % 2 * shard, (i % 2 + 1) * shard)
            out[...] = (total[:, cut] + other[i % 2].astype(F32)).astype(out.dtype)


def projected(at, flags, grads, first, second, other=None):
    count = len(grads) // 3
    rows, width = grads[0].shape
    shard = first.shape[1]
    moving = pl.BlockSpec((2, count * rows, shard), lambda i, at, flags: (i, 0, 0))
    fixed = pl.BlockSpec((count * rows, shard), lambda i, at, flags: (0, 0))
    if other is None:
        kernel, extra = give_kernel, ()
        out_specs = moving
        out_shape = jax.ShapeDtypeStruct((4, count * rows, shard), BF16)
    else:
        kernel, extra = keep_kernel, (other,)
        out_specs = [fixed] * 4
        out_shape = [
            jax.ShapeDtypeStruct((count * rows, shard), t) for t in (BF16, BF16, BF16, F32)
        ]
    return pl.pallas_call(
        functools.partial(kernel, count),
        grid_spec=pltpu.PrefetchScalarGridSpec(
            num_scalar_prefetch=2,
            grid=(2,),
            in_specs=[HBM] * (len(grads) + 2) + [moving] * len(extra),
            out_specs=out_specs,
            scratch_shapes=[
                pltpu.VMEM((count * rows, 2 * shard), F32),
                pltpu.VMEM((2, count * rows, width), BF16),
                pltpu.SemaphoreType.DMA((2, count)),
                pltpu.VMEM((2, 4, shard, width), BF16),
                pltpu.SemaphoreType.DMA((2, 4)),
            ],
        ),
        out_shape=out_shape,
        cost_estimate=cost(
            2 * count * rows * 2 * width * 4 * shard, 2 * 2 * 4 * shard * width
        ),
    )(at, flags, *grads, first, second, *extra)


def per_device(out_grad, queries, enc_keys, enc_values, key_mask, weights):
    decoder = lax.axis_index("section") == 1
    half = lax.axis_index("fsdp") % 2
    segment = lax.axis_index("segment")
    core = segment % 2
    chip = segment // 2
    micro_count, reaction_count, seq_length, feature_width = out_grad.shape
    local_width = queries.shape[3]
    shard_rows = weights.shape[2]
    row_count = micro_count * reaction_count * seq_length
    flat = (micro_count, seq_length, local_width)
    micros = range(micro_count)
    dec = decoder.astype(jnp.int32)

    def gathered(shard):
        return lax.all_gather(shard, "fsdp", axis=0, axis_index_groups=Z_LINES)

    own = (
        queries.reshape(flat),
        enc_keys.reshape(flat),
        enc_values.reshape(flat),
        jnp.broadcast_to(
            jnp.where(key_mask > 0, 0.0, -jnp.inf).astype(F32).reshape(micro_count, seq_length, 1),
            (micro_count, seq_length, HDIM),
        ),
    )
    came_near = []
    for value in own:
        came_near.append(lax.ppermute(value, BOTH, ENC_SWAP))
    near = [jnp.where(decoder, mine, other) for mine, other in zip(own, came_near)]
    near_flags = jnp.stack([dec, 1 - dec])
    own_flags = jnp.stack([0 * dec, 1 - dec])
    far_scalars, near_scalars = jnp.stack([core, dec]), jnp.stack([half, dec])
    places = 2 * ((chip + jnp.array(STEPS, jnp.int32)) % 4)
    keep_at, give_at = places + core, places + 1 - core

    grads = out_grad.reshape(row_count, feature_width)
    columns = 2 * (4 * core + jnp.arange(4, dtype=jnp.int32)) + 1 - half
    first = gathered(weights[0, 0])
    part = picked(grads, columns, shard_rows)
    part, later_weights = lax.optimization_barrier((part, weights))
    second = gathered(later_weights[0, 1])
    came = lax.ppermute(part, BOTH, DEC_SWAP)
    twin = lax.ppermute(came, "segment", CORE_SWAP)

    ready = (came, twin, near, own[3], near_flags, own_flags, keep_at, give_at)
    ready = (*ready, far_scalars, near_scalars)
    first, ready = lax.optimization_barrier((first, ready))
    came, twin, near, own_mask, near_flags, own_flags, keep_at, give_at, *scalars = ready
    far_scalars, near_scalars = scalars
    own = (*own[:3], own_mask)

    piece = 2 * shard_rows
    moved = pl.BlockSpec((row_count, piece), lambda j, at: (0, j % 2))
    far = []
    for partial in partial_products(far_scalars, (came, twin), [moved] * 2, first, BF16, far_kernel):
        far.append(lax.ppermute(partial, BOTH, DEC_SWAP))
    own_partial = partial_products(
        near_scalars,
        (grads, grads),
        [
            pl.BlockSpec((row_count, shard_rows), lambda j, half: (0, 4 * j + half[0])),
            pl.BlockSpec((row_count, shard_rows), lambda j, half: (0, 4 * j + 2 + half[0])),
        ],
        first,
        F32,
        near_kernel,
    )
    ctx, ctx_near, ctx_own = [], [], []
    for micro in micros:
        part = far[micro]
        if micro > 0:
            part, ctx[-1] = lax.optimization_barrier((part, ctx[-1]))
        ctx.append((own_partial[micro] + part.astype(F32)).astype(BF16))
        ctx_near.append(lax.ppermute(ctx[micro], BOTH, DEC_TO_ENC))
        ctx_own.append(lax.ppermute(ctx_near[micro], BOTH, ENC_SWAP))

    def attended(flags, sent, held, operands):
        grads = []
        for micro in micros:
            came = sent[micro]
            if micro > 0:
                came, grads[-1] = lax.optimization_barrier((came, grads[-1]))
            grads.append(attend(flags, (came, *held[micro : micro + 1]), *operands, micro))
        return zip(*grads)

    dk, dv = attended(near_flags, ctx_near, ctx, near)
    far_dq = []
    for micro in micros:
        far_dq.append(lax.ppermute(dv[micro], BOTH, DEC_SWAP))
    own_dk, own_dv = attended(own_flags, ctx_own, (), own)

    second, own_dk, own_dv = lax.optimization_barrier((second, own_dk, own_dv))

    def chip_sums(grads):
        give = projected(give_at, dec[None], grads, first, second)
        other = lax.ppermute(give, "segment", CORE_SWAP)
        return projected(keep_at, dec[None], grads, first, second, other)

    def reduced(blocks, result):
        for step, block in zip(STEPS, blocks):
            pairs = [(2 * x + k, 2 * ((x + step) % 4) + k) for x in range(4) for k in range(2)]
            other = lax.ppermute(block, "segment", pairs)
            result = result + other.astype(F32)
        return result.astype(BF16)

    *blocks, block = chip_sums((*far_dq, *dk, *dv))
    from_partner = lax.ppermute(reduced(blocks, block), "fsdp", HALF_SWAP)
    *blocks, block = chip_sums((*dv, *own_dk, *own_dv))
    own_out = reduced(blocks, block)
    result = jnp.where(
        half == 0,
        jnp.concatenate([own_out, from_partner], axis=1),
        jnp.concatenate([from_partner, own_out], axis=1),
    )
    return result.reshape(1, micro_count, reaction_count, seq_length, 2 * shard_rows)


def solution(mesh):
    return jax.shard_map(
        per_device,
        mesh=mesh,
        in_specs=(
            P(None, "fsdp", None, None),
            P(None, "fsdp", None, "segment"),
            P(None, "fsdp", None, "segment"),
            P(None, "fsdp", None, "segment"),
            P(None, "fsdp", None),
            P("section", None, "fsdp", "segment"),
        ),
        out_specs=P("section", None, "fsdp", None, "segment"),
        check_vma=False,
    )
```

```python
import functools

import jax
import jax.numpy as jnp
from jax import lax
from jax.experimental import pallas as pl
from jax.experimental.pallas import tpu as pltpu
from jax.sharding import PartitionSpec as P


HDIM = 128

Z_LINES = [[2 * z + half for z in range(8)] for half in range(2)]
DEC_SWAP = [(16 + f, 16 + (f ^ 1)) for f in range(16)]
ENC_SWAP = [(f, f ^ 1) for f in range(16)]
DEC_TO_ENC = [(16 + f, f ^ 1) for f in range(16)]
HALF_SWAP = [(f, f ^ 1) for f in range(16)]
CORE_SWAP = [(g, g ^ 1) for g in range(8)]
BOTH = ("section", "fsdp")
STEPS = (2, 1, 3, 0)
F32 = jnp.float32
SMALL = pltpu.CompilerParams(vmem_limit_bytes=20 * 2**20)
HBM = pl.BlockSpec(memory_space=pltpu.HBM)
BF16 = jnp.bfloat16
NT = (((1,), (1,)), ((), ()))
TN = (((0,), (0,)), ((), ()))
NN = (((1,), (0,)), ((), ()))


def mm(left, right, dims):
    return lax.dot_general(left, right, dims, preferred_element_type=F32)


def cost(flops, bytes_accessed):
    return pl.CostEstimate(flops=flops, bytes_accessed=bytes_accessed, transcendentals=0)


def pick_kernel(where, source, target):
    target[...] = source[...]


def picked(source, columns, width):
    rows = source.shape[0]
    count = columns.shape[0]
    return pl.pallas_call(
        pick_kernel,
        grid_spec=pltpu.PrefetchScalarGridSpec(
            num_scalar_prefetch=1,
            grid=(count,),
            in_specs=[pl.BlockSpec((rows, width), lambda i, at: (0, at[i]))],
            out_specs=pl.BlockSpec((rows, width), lambda i, at: (0, i)),
        ),
        out_shape=jax.ShapeDtypeStruct((rows, count * width), source.dtype),
        cost_estimate=cost(0, 2 * rows * count * width * 2),
        name="pick",
    )(columns, source)


def fetched(step, weight, buffer, sems):
    rows = weight.shape[1]
    copies = [
        pltpu.make_async_copy(weight.at[z], buffer.at[pl.ds(z * rows, rows)], sems.at[z])
        for z in range(8)
    ]

    @pl.when(step == 0)
    def _():
        for copy in copies:
            copy.start()

    for j in range(4):

        @pl.when(step == j)
        def _():
            copies[2 * j].wait()
            copies[2 * j + 1].wait()

    return buffer[pl.ds(pl.multiple_of(step * 2 * rows, 2 * rows), 2 * rows), :]


def added(step, acc, part):
    @pl.when(step == 0)
    def _():
        acc[...] = part

    @pl.when(step > 0)
    def _():
        acc[...] += part


def far_kernel(scalars, came, twin, weight, low, high, acc, buffer, sems):
    step = pl.program_id(0)

    @pl.when(scalars[1] > 0)
    def _():
        rows = jnp.where(scalars[0] == step // 2, came[...], twin[...])
        added(step, acc, mm(rows, fetched(step, weight, buffer, sems), NN))

        @pl.when(step == pl.num_programs(0) - 1)
        def _():
            count = low.shape[0]
            low[...] = acc[:count].astype(BF16)
            high[...] = acc[count:].astype(BF16)


def near_kernel(scalars, first, second, weight, low, high, buffer, sems):
    step = pl.program_id(0)

    @pl.when(scalars[1] > 0)
    def _():
        rows = jnp.concatenate([first[...], second[...]], axis=1)
        part = mm(rows, fetched(step, weight, buffer, sems), NN)
        count = low.shape[0]
        added(step, low, part[:count])
        added(step, high, part[count:])


def partial_products(scalars, operands, specs, weight, out_dtype, kernel):
    row_count = operands[0].shape[0]
    _, shard, width = weight.shape
    extra = [pltpu.VMEM((row_count, width), F32)] if out_dtype == BF16 else []
    return pl.pallas_call(
        kernel,
        grid_spec=pltpu.PrefetchScalarGridSpec(
            num_scalar_prefetch=1,
            grid=(4,),
            in_specs=specs + [HBM],
            out_specs=[pl.BlockSpec((row_count // 2, width), lambda j, at: (0, 0))] * 2,
            scratch_shapes=extra
            + [pltpu.VMEM((8 * shard, width), BF16), pltpu.SemaphoreType.DMA((8,))],
        ),
        out_shape=[jax.ShapeDtypeStruct((row_count // 2, width), out_dtype)] * 2,
        cost_estimate=cost(2 * row_count * 8 * shard * width, 2 * 8 * shard * width),
    )(scalars, *operands, weight)


def attend_kernel(heads, flags, *refs):
    *sent, query, key, value, hidden, first_out, second_out = refs
    scale = HDIM ** (-0.5)
    cuts = [slice(head * HDIM, (head + 1) * HDIM) for head in range(heads)]

    def grads_of(cut):
        grad = sent[0][:, cut]
        if len(sent) > 1:
            grad = jnp.where(flags[0] > 0, sent[1][:, cut], grad)
        q, k, v = query[:, cut], key[:, cut], value[:, cut]
        scores = mm(k, q, NT) * scale + jnp.concatenate([hidden[...]] * 2, axis=1)
        prob_grad = mm(v, grad, NT)
        raised = jnp.exp(scores - jnp.max(scores, axis=0, keepdims=True))
        share = 1.0 / jnp.sum(raised, axis=0, keepdims=True)
        center = jnp.sum(raised * prob_grad, axis=0, keepdims=True) * share
        probs = raised * share
        return grad, q, k, probs, (probs * (prob_grad - center)).astype(BF16)

    def query_grads():
        for cut in cuts:
            _, _, k, _, score_grad = grads_of(cut)
            second_out[:, cut] = (mm(score_grad, k, TN) * scale).astype(BF16)

    def key_value_grads():
        for cut in cuts:
            grad, q, _, probs, score_grad = grads_of(cut)
            first_out[:, cut] = (mm(score_grad, q, NN) * scale).astype(BF16)
            second_out[:, cut] = mm(probs.astype(BF16), grad, NN).astype(BF16)

    if len(sent) > 1:
        pl.when(flags[0] > 0)(query_grads)
    pl.when(flags[1] > 0)(key_value_grads)


def attend(flags, sent, query, key, value, mask, micro):
    seq_length, width = sent[0].shape
    heads = 2
    wide = heads * HDIM
    one = pl.BlockSpec((seq_length, wide), lambda h, flags: (0, h))
    row = pl.BlockSpec((None, seq_length, wide), lambda h, flags: (micro, 0, h))
    out = jax.ShapeDtypeStruct((seq_length, width), BF16)
    taken = [one]
    if len(sent) > 1:
        taken = [
            pl.BlockSpec((seq_length, wide), lambda h, flags: (0, h * flags[1])),
            pl.BlockSpec((seq_length, wide), lambda h, flags: (0, h * flags[0])),
        ]
    return pl.pallas_call(
        functools.partial(attend_kernel, heads),
        grid_spec=pltpu.PrefetchScalarGridSpec(
            num_scalar_prefetch=1,
            grid=(width // wide,),
            in_specs=taken
            + [
                row,
                row,
                row,
                pl.BlockSpec((None, seq_length, HDIM), lambda h, flags: (micro, 0, 0)),
            ],
            out_specs=[one] * 2,
        ),
        out_shape=[out] * 2,
        cost_estimate=cost(
            10 * seq_length * seq_length * width, 16 * seq_length * width
        ),
        compiler_params=SMALL,
        name="attend",
    )(flags, *sent, query, key, value, mask)


def products(count, at, flags, refs):
    kinds = [refs[kind * count : (kind + 1) * count] for kind in range(3)]
    weights = refs[3 * count : 3 * count + 2]
    total, rows, row_sems, buffer, sems = refs[-5:]
    each = rows.shape[1] // count
    step = pl.program_id(0)
    encoder = flags[0] == 0

    def row_copy(kind, which, i):
        return pltpu.make_async_copy(
            kinds[kind][i], rows.at[which, pl.ds(i * each, each)], row_sems.at[which, i]
        )

    def copy(which, place):
        return pltpu.make_async_copy(
            weights[which].at[at[place]], buffer.at[which, place], sems.at[which, place]
        )

    def wide(which):
        pair = buffer[which, pl.ds(2 * step, 2)]
        return pair.reshape(pair.shape[0] * pair.shape[1], pair.shape[2])

    @pl.when((step == 0) & encoder)
    def _():
        for turn in range(2):
            for which, kind in ((1, 2), (0, 1)):
                for i in range(count if turn == 0 else 0):
                    row_copy(kind, which, i).start()
                copy(which, 2 * turn).start()
                copy(which, 2 * turn + 1).start()
        for i in range(count):
            row_copy(2, 1, i).wait()

    @pl.when((step == 0) & (flags[0] > 0))
    def _():
        for i in range(count):
            row_copy(0, 1, i).start()
        for place in range(4):
            copy(1, place).start()
        for i in range(count):
            row_copy(0, 1, i).wait()

    copy(1, 2 * step).wait()
    copy(1, 2 * step + 1).wait()
    total[...] = mm(rows[1], wide(1), NT)

    @pl.when((step == 0) & encoder)
    def _():
        for i in range(count):
            row_copy(1, 0, i).wait()

    @pl.when(encoder)
    def _():
        copy(0, 2 * step).wait()
        copy(0, 2 * step + 1).wait()
        total[...] += mm(rows[0], wide(0), NT)

    return total


def give_kernel(count, at, flags, *refs):
    out = refs[3 * count + 2]
    total = products(count, at, flags, refs)
    shard = out.shape[2]
    for place in range(2):
        out[place] = total[:, place * shard : (place + 1) * shard].astype(BF16)


def keep_kernel(count, at, flags, *refs):
    other, outs = refs[3 * count + 2], refs[3 * count + 3 : 3 * count + 7]
    total = products(count, at, flags, refs)
    shard = outs[0].shape[1]
    for i, out in enumerate(outs):

        @pl.when(pl.program_id(0) == i // 2)
        def _():
            cut = slice(i % 2 * shard, (i % 2 + 1) * shard)
            out[...] = (total[:, cut] + other[i % 2].astype(F32)).astype(out.dtype)


def projected(at, flags, grads, first, second, other=None):
    count = len(grads) // 3
    rows, width = grads[0].shape
    shard = first.shape[1]
    moving = pl.BlockSpec((2, count * rows, shard), lambda i, at, flags: (i, 0, 0))
    fixed = pl.BlockSpec((count * rows, shard), lambda i, at, flags: (0, 0))
    if other is None:
        kernel, extra = give_kernel, ()
        out_specs = moving
        out_shape = jax.ShapeDtypeStruct((4, count * rows, shard), BF16)
    else:
        kernel, extra = keep_kernel, (other,)
        out_specs = [fixed] * 4
        out_shape = [
            jax.ShapeDtypeStruct((count * rows, shard), t) for t in (BF16,) * 4
        ]
    return pl.pallas_call(
        functools.partial(kernel, count),
        grid_spec=pltpu.PrefetchScalarGridSpec(
            num_scalar_prefetch=2,
            grid=(2,),
            in_specs=[HBM] * (len(grads) + 2) + [moving] * len(extra),
            out_specs=out_specs,
            scratch_shapes=[
                pltpu.VMEM((count * rows, 2 * shard), F32),
                pltpu.VMEM((2, count * rows, width), BF16),
                pltpu.SemaphoreType.DMA((2, count)),
                pltpu.VMEM((2, 4, shard, width), BF16),
                pltpu.SemaphoreType.DMA((2, 4)),
            ],
        ),
        out_shape=out_shape,
        cost_estimate=cost(
            2 * count * rows * 2 * width * 4 * shard, 2 * 2 * 4 * shard * width
        ),
    )(at, flags, *grads, first, second, *extra)


def per_device(out_grad, queries, enc_keys, enc_values, key_mask, weights):
    decoder = lax.axis_index("section") == 1
    half = lax.axis_index("fsdp") % 2
    segment = lax.axis_index("segment")
    core = segment % 2
    chip = segment // 2
    micro_count, reaction_count, seq_length, feature_width = out_grad.shape
    local_width = queries.shape[3]
    shard_rows = weights.shape[2]
    row_count = micro_count * reaction_count * seq_length
    flat = (micro_count, seq_length, local_width)
    micros = range(micro_count)
    dec = decoder.astype(jnp.int32)

    def gathered(shard):
        return lax.all_gather(shard, "fsdp", axis=0, axis_index_groups=Z_LINES)

    own = (
        queries.reshape(flat),
        enc_keys.reshape(flat),
        enc_values.reshape(flat),
        jnp.broadcast_to(
            jnp.where(key_mask > 0, 0.0, -jnp.inf).astype(F32).reshape(micro_count, seq_length, 1),
            (micro_count, seq_length, HDIM),
        ),
    )
    came_near = []
    for value in own:
        came_near.append(lax.ppermute(value, BOTH, ENC_SWAP))
    near = [jnp.where(decoder, mine, other) for mine, other in zip(own, came_near)]
    near_flags = jnp.stack([dec, 1 - dec])
    own_flags = jnp.stack([0 * dec, 1 - dec])
    far_scalars, near_scalars = jnp.stack([core, dec]), jnp.stack([half, dec])
    places = 2 * ((chip + jnp.array(STEPS, jnp.int32)) % 4)
    keep_at, give_at = places + core, places + 1 - core

    grads = out_grad.reshape(row_count, feature_width)
    columns = 2 * (4 * core + jnp.arange(4, dtype=jnp.int32)) + 1 - half
    first = gathered(weights[0, 0])
    part = picked(grads, columns, shard_rows)
    part, later_weights = lax.optimization_barrier((part, weights))
    second = gathered(later_weights[0, 1])
    came = lax.ppermute(part, BOTH, DEC_SWAP)
    twin = lax.ppermute(came, "segment", CORE_SWAP)

    ready = (came, twin, near, own[3], near_flags, own_flags, keep_at, give_at)
    ready = (*ready, far_scalars, near_scalars)
    first, ready = lax.optimization_barrier((first, ready))
    came, twin, near, own_mask, near_flags, own_flags, keep_at, give_at, *scalars = ready
    far_scalars, near_scalars = scalars
    own = (*own[:3], own_mask)

    piece = 2 * shard_rows
    moved = pl.BlockSpec((row_count, piece), lambda j, at: (0, j % 2))
    far = []
    for partial in partial_products(far_scalars, (came, twin), [moved] * 2, first, BF16, far_kernel):
        far.append(lax.ppermute(partial, BOTH, DEC_SWAP))
    own_partial = partial_products(
        near_scalars,
        (grads, grads),
        [
            pl.BlockSpec((row_count, shard_rows), lambda j, half: (0, 4 * j + half[0])),
            pl.BlockSpec((row_count, shard_rows), lambda j, half: (0, 4 * j + 2 + half[0])),
        ],
        first,
        F32,
        near_kernel,
    )
    ctx, ctx_near, ctx_own = [], [], []
    for micro in micros:
        part = far[micro]
        if micro > 0:
            part, ctx[-1] = lax.optimization_barrier((part, ctx[-1]))
        ctx.append((own_partial[micro] + part.astype(F32)).astype(BF16))
        ctx_near.append(lax.ppermute(ctx[micro], BOTH, DEC_TO_ENC))
        ctx_own.append(lax.ppermute(ctx_near[micro], BOTH, ENC_SWAP))

    def attended(flags, sent, held, operands):
        grads = []
        for micro in micros:
            came = sent[micro]
            if micro > 0:
                came, grads[-1] = lax.optimization_barrier((came, grads[-1]))
            grads.append(attend(flags, (came, *held[micro : micro + 1]), *operands, micro))
        return zip(*grads)

    dk, dv = attended(near_flags, ctx_near, ctx, near)
    far_dq = []
    for micro in micros:
        far_dq.append(lax.ppermute(dv[micro], BOTH, DEC_SWAP))
    own_dk, own_dv = attended(own_flags, ctx_own, (), own)

    second, own_dk, own_dv = lax.optimization_barrier((second, own_dk, own_dv))

    def chip_sums(grads):
        give = projected(give_at, dec[None], grads, first, second)
        other = lax.ppermute(give, "segment", CORE_SWAP)
        return projected(keep_at, dec[None], grads, first, second, other)

    def reduced(blocks, result):
        result = result.astype(F32)
        for step, block in zip(STEPS, blocks):
            pairs = [(2 * x + k, 2 * ((x + step) % 4) + k) for x in range(4) for k in range(2)]
            other = lax.ppermute(block, "segment", pairs)
            result = result + other.astype(F32)
        return result.astype(BF16)

    *blocks, block = chip_sums((*far_dq, *dk, *dv))
    from_partner = lax.ppermute(reduced(blocks, block), "fsdp", HALF_SWAP)
    *blocks, block = chip_sums((*dv, *own_dk, *own_dv))
    own_out = reduced(blocks, block)
    result = jnp.where(
        half == 0,
        jnp.concatenate([own_out, from_partner], axis=1),
        jnp.concatenate([from_partner, own_out], axis=1),
    )
    return result.reshape(1, micro_count, reaction_count, seq_length, 2 * shard_rows)


def solution(mesh):
    return jax.shard_map(
        per_device,
        mesh=mesh,
        in_specs=(
            P(None, "fsdp", None, None),
            P(None, "fsdp", None, "segment"),
            P(None, "fsdp", None, "segment"),
            P(None, "fsdp", None, "segment"),
            P(None, "fsdp", None),
            P("section", None, "fsdp", "segment"),
        ),
        out_specs=P("section", None, "fsdp", None, "segment"),
        check_vma=False,
    )
```
